32 devices in a mesh: row: 2 (over x), feat: 16 (over z, y, core).
Axes of the slice: x: 2, y: 2, z: 4, core: 2. Of those that a mesh axis runs over, the one named last changes fastest.
Arguments:
- logits: bfloat16 [2048, 1000], P(('row', 'feat')), may hold values from -200 to 200, as said below
- labels: int32 [2048], P(('row', 'feat')), may hold values from 0 to 999
- projection: bfloat16 [1000, 16], replicated, may hold values from -4 to 4
- bins: int32 [2048, 2048], P('feat', 'row'), may hold values from 0 to 63, as said below
- nbins: int32 [2048], P('feat'), may hold values from 2 to 64
- leaf: int32 [2048], P('row'), may hold values from 0 to 15
Outputs:
- relative_gain: float32 [16, 131072], P('row', 'feat')
The draws below stay inside these ranges and needn't reach their ends.
Inputs may be any that keep to these rules, and one draw needn't show every extreme that they name: `logits`: shows the class scores; some rows may lie far from zero. bins[f, i] < nbins[f].
All inputs are finite; a program needn't handle non-finite values.
Results may differ from the reference program's by a relative error of at most 0.0017.
Values may be sent and summed in bfloat16 or wider, within the bound.
No kernel may reach another device: no remote copies, remote signals or barrier semaphores. Data moves between devices by JAX's collectives and lax.ppermute only.
A program may use at most 64 MiB of HBM per device.

```python
import math
import jax
import jax.numpy as jnp
from jax import lax

C = 1000
F = 2048
K = 16
BINS = 64
LEAVES = 16
ROWS = 2048
N_ROW = 2


def draw_logits(key, part):
    first = jax.random.fold_in(jax.random.fold_in(key, 3), 0)
    return (jax.random.normal(first, (ROWS, C), jnp.float32) * 3.0).astype(jnp.bfloat16)


def bin_counts(key):
    first, second = jax.random.split(jax.random.fold_in(key, 11))
    caps = jax.random.randint(first, (F // 32, 1), 4, BINS + 1)
    counts = jax.random.randint(second, (F // 32, 32), 2, BINS + 1)
    return jnp.minimum(counts, caps).reshape(F)


def draw_nbins(key, part):
    return bin_counts(key)


def draw_bins(key, part):
    counts = bin_counts(key)
    raw = jax.random.randint(jax.random.fold_in(key, 17), (F, ROWS), 0, 1 << 20)
    return raw % counts[:, None]


def place_ends(values, rng, least, high):
    spot = [jax.random.randint(jax.random.fold_in(rng, axis), (), 0, length) for axis, length in enumerate(values.shape)]
    longest = values.shape.index(max(values.shape))
    beside = spot[:longest] + [(spot[longest] + 1) % values.shape[longest]] + spot[longest + 1:]
    return values.at[tuple(spot)].set(least).at[tuple(beside)].set(high)


def normal_values(stream_key, dims, deviation, limit, kind=jnp.bfloat16):
    array = jax.random.normal(stream_key, dims, jnp.float32) * deviation
    return jnp.minimum(jnp.maximum(array, -limit), limit).astype(kind)


def setup_inputs(seed: int = 0) -> dict:
    key_of = jax.random.split(jax.random.key(seed), 7)
    logits = draw_logits(jax.random.fold_in(key_of[6], 71), 0)
    labels = place_ends(jax.random.randint(key_of[1], (ROWS,), 0, C), jax.random.fold_in(key_of[1], 1), 0, C - 1).astype(jnp.int32)
    projection = normal_values(key_of[2], (C, K), 1.0, 4.0)
    bins = draw_bins(jax.random.fold_in(key_of[6], 71), 0)
    nbins = draw_nbins(jax.random.fold_in(key_of[6], 71), 0)
    leaf = place_ends(jax.random.randint(key_of[5], (ROWS,), 0, LEAVES), jax.random.fold_in(key_of[5], 1), 0, LEAVES - 1).astype(jnp.int32)
    return dict(logits=logits, labels=labels, projection=projection, bins=bins, nbins=nbins, leaf=leaf)


ridge = 1.0
epsilon = 1e-6


def row_values(logits, labels, projection):
    scores = logits.astype(jnp.float32)
    highest = jnp.max(scores, axis=1, keepdims=True)
    expd = jnp.exp(scores - highest)
    probability = expd / jnp.sum(expd, axis=1, keepdims=True)
    classes = jnp.arange(logits.shape[1], dtype=jnp.int32)
    target = (labels[:, None] == classes[None, :]).astype(jnp.float32)
    gradient = (probability - target).astype(jnp.bfloat16)
    sketch = jnp.dot(gradient, projection, preferred_element_type=jnp.float32).astype(jnp.bfloat16)
    hessian = jnp.sum(probability * (1.0 - probability), axis=1).astype(jnp.bfloat16)
    return jnp.concatenate([sketch, hessian[:, None]], axis=1).astype(jnp.float32)


def shard_histogram(values, leaf_rows, bin_rows):
    rows = values.shape[0]
    width = math.gcd(F, 256)
    groups = F // width
    columns = values.shape[1]
    grouped = bin_rows.reshape(rows, groups, width).transpose(1, 0, 2)
    offsets = jnp.arange(width, dtype=jnp.int32)
    spread = jnp.broadcast_to(values[:, None, :], (rows, width, columns)).reshape(rows * width, columns)

    def one_group(group_bins):
        segment = ((offsets[None, :] * BINS + group_bins) * LEAVES + leaf_rows[:, None]).reshape(-1)
        summed = jax.ops.segment_sum(spread, segment.astype(jnp.int32), num_segments=width * BINS * LEAVES)
        return summed.reshape(width, BINS, LEAVES, columns)

    stacked = lax.map(one_group, grouped)
    return stacked.reshape(F, BINS, LEAVES, columns)


def split_gains(histogram, nbins):
    left = jnp.cumsum(histogram, axis=3)
    total = left[..., -1:]
    right = total - left

    def score(sums):
        return jnp.sum(sums[:, :-1] * sums[:, :-1] / (sums[:, -1:] + ridge), axis=1)

    gain = score(left) + score(right) - score(total)
    valid = jnp.arange(histogram.shape[3], dtype=jnp.int32)[None, :] < (nbins[:, None] - 1)
    return jnp.where(valid[None], gain, jnp.zeros_like(gain))


def reference(logits, labels, projection, bins, nbins, leaf):
    values = row_values(logits, labels, projection)
    shard_rows = ROWS // N_ROW
    total = jnp.zeros((F, BINS, LEAVES, K + 1), jnp.float32)
    for shard in range(N_ROW):
        low = shard * shard_rows
        part = shard_histogram(values[low:low + shard_rows], leaf[low:low + shard_rows], bins[:, low:low + shard_rows].T)
        total = total + part
    histogram = total.transpose(2, 3, 0, 1)
    gain = split_gains(histogram, nbins)
    best = jnp.max(gain, axis=(1, 2))
    relative = gain / (best[:, None, None] + epsilon)
    return relative.reshape(LEAVES, F * BINS)
```

```python
import functools

import jax
import jax.numpy as jnp
from jax import lax
from jax.experimental import pallas as pl
from jax.experimental.pallas import tpu as pltpu
from jax.sharding import PartitionSpec as P

BINS = 64
LEAVES = 16
LANES = 128
ridge = 1.0
epsilon = 1e-06


def vmem():
    return pl.BlockSpec(memory_space=pltpu.VMEM)


def narrow_kernel(bins_ref, leaf_ref, out_ref):
    features = bins_ref.shape[0]
    out_ref[:features, :] = bins_ref[...].astype(jnp.float32).astype(jnp.bfloat16)
    tail = out_ref.shape[0] - features
    leaf = jnp.broadcast_to(leaf_ref[...].astype(jnp.float32), (tail, leaf_ref.shape[1]))
    out_ref[features:, :] = leaf.astype(jnp.bfloat16)


def narrow(bins, leaf):
    features, rows = bins.shape
    return pl.pallas_call(
        narrow_kernel,
        out_shape=jax.ShapeDtypeStruct((features + 16, rows), jnp.bfloat16),
        in_specs=[vmem(), vmem()],
        out_specs=vmem(),
        name="narrow",
    )(bins, leaf.reshape(1, rows))


def gradient_kernel(logits_ref, labels_ref, projection_ref, out_ref):
    rows, classes = logits_ref.shape
    scores = logits_ref[...].astype(jnp.float32)
    highest = jnp.max(scores, axis=1, keepdims=True)
    expd = jnp.exp(scores - highest)
    probability = expd / jnp.sum(expd, axis=1, keepdims=True)
    labels = jnp.broadcast_to(labels_ref[...].astype(jnp.float32), (LANES, rows))
    labels = jnp.transpose(labels)[:, :1].astype(jnp.int32)
    lane = lax.broadcasted_iota(jnp.int32, (rows, classes), 1)
    target = jnp.where(lane == labels, 1.0, 0.0)
    gradient = (probability - target).astype(jnp.bfloat16)
    sketch = lax.dot_general(
        projection_ref[...], gradient, (((1,), (1,)), ((), ())), preferred_element_type=jnp.float32
    )
    hessian = jnp.sum(probability * (1.0 - probability), axis=1, keepdims=True)
    hessian = jnp.transpose(jnp.broadcast_to(hessian, (rows, LANES)))[:8, :]
    top = jnp.concatenate([sketch[:8], hessian], axis=0)
    low = jnp.concatenate([sketch[8:], jnp.zeros_like(hessian)], axis=0)
    packed = jnp.concatenate([top, low], axis=1).astype(jnp.bfloat16)
    out_ref[...] = jnp.broadcast_to(packed[None], out_ref.shape)


def gradient_values(logits, labels, projection, copies):
    rows, _ = logits.shape
    return pl.pallas_call(
        gradient_kernel,
        out_shape=jax.ShapeDtypeStruct((copies, 16, 2 * rows), jnp.bfloat16),
        in_specs=[vmem(), vmem(), vmem()],
        out_specs=vmem(),
        name="gradient",
    )(logits, labels.reshape(1, rows), projection.T)


def gain_kernel(n_row, share, group, values_ref, nbins_ref, *refs):
    bins_refs, (gain_ref, best_ref), (weights,) = refs[:n_row], refs[n_row : n_row + 2], refs[n_row + 2 :]
    features = bins_refs[0].shape[0] - 16
    rows = bins_refs[0].shape[1]
    sources = values_ref.shape[0] // n_row
    half = values_ref.shape[2] // 2
    me = lax.axis_index("row")
    wide = (share, LANES)
    my_leaf = lax.broadcasted_iota(jnp.int32, wide, 0) + me * share
    my_leaf = my_leaf.astype(jnp.float32)
    left_half = lax.broadcasted_iota(jnp.int32, (16, LANES), 1) < half
    totals = [jnp.zeros(wide, jnp.float32) for _ in range(17)]
    for s in range(n_row):
        shard = lax.rem(me + s, n_row)
        for pair in range(sources // 2):
            first = values_ref[shard * sources + 2 * pair].astype(jnp.float32)
            second = values_ref[shard * sources + 2 * pair + 1].astype(jnp.float32)
            top = jnp.where(left_half, first, pltpu.roll(second, half, 1))
            low = jnp.where(left_half, pltpu.roll(first, half, 1), second)
            cols = slice(pair * LANES, (pair + 1) * LANES)
            leaf = bins_refs[s][features : features + 16, cols].astype(jnp.float32)[:1]
            mine = jnp.broadcast_to(leaf, wide) == my_leaf
            pieces = []
            for k in range(17):
                row = top[k : k + 1] if k < 8 else low[k - 8 : k - 7] if k < 16 else top[8:9]
                piece = jnp.where(mine, jnp.broadcast_to(row, wide), 0.0)
                totals[k] = totals[k] + piece
                pieces.append(piece)
            pieces.append(jnp.zeros(wide, jnp.float32))
            weights[:, s * rows + pair * LANES : s * rows + (pair + 1) * LANES] = jnp.concatenate(
                pieces, axis=0
            ).astype(jnp.bfloat16)
    totals = [jnp.broadcast_to(jnp.sum(t, axis=1, keepdims=True), wide) for t in totals]

    def score(sums):
        squares = sums[0] * sums[0]
        for k in range(1, 16):
            squares = squares + sums[k] * sums[k]
        return squares / (sums[16] + ridge)

    of_all = score(totals)
    bin_id = lax.broadcasted_iota(jnp.int32, (BINS, LANES), 0).astype(jnp.float32)
    bin_id = bin_id.astype(jnp.bfloat16)
    lane = lax.broadcasted_iota(jnp.int32, wide, 1)
    one, zero = jnp.bfloat16(1.0), jnp.bfloat16(0.0)

    def add_group(g, best):
        start = pl.multiple_of(g * group, group)
        tables = []
        for s in range(n_row):
            block = bins_refs[s][pl.ds(start, group), :]
            columns = []
            for j in range(group):
                line = block[j : j + 1]
                blocks = []
                for c in range(rows // LANES):
                    at = jnp.broadcast_to(line[:, c * LANES : (c + 1) * LANES], (BINS, LANES))
                    blocks.append(jnp.where(at <= bin_id, one, zero))
                columns.append(jnp.concatenate(blocks, axis=1))
            tables.append(jnp.concatenate(columns, axis=0))
        sums = None
        for s in range(n_row):
            part = lax.dot_general(
                weights[:, s * rows : (s + 1) * rows],
                tables[s],
                (((1,), (1,)), ((), ())),
                preferred_element_type=jnp.float32,
            )
            sums = part if sums is None else sums + part
        for c in range(group * BINS // LANES):
            left = [sums[k * share : (k + 1) * share, c * LANES : (c + 1) * LANES] for k in range(17)]
            right = [totals[k] - left[k] for k in range(17)]
            gain = score(left) + score(right) - of_all
            a = nbins_ref[start + 2 * c] - 1
            b = nbins_ref[start + 2 * c + 1] - 1 + BINS
            last = jnp.where(lane < BINS, a, b)
            gain = jnp.where(lane < last, gain, 0.0)
            gain_ref[:, pl.ds(pl.multiple_of(start * BINS + c * LANES, LANES), LANES)] = gain
            best = jnp.maximum(best, gain)
        return best

    best = lax.fori_loop(0, features // group, add_group, jnp.full(wide, -jnp.inf, jnp.float32))
    best_ref[...] = jnp.broadcast_to(jnp.max(best, axis=1, keepdims=True), wide)


def split_gains(values, nbins, bins, n_row):
    share = LEAVES // n_row
    features, rows = bins[0].shape[0] - 16, bins[0].shape[1]
    return pl.pallas_call(
        functools.partial(gain_kernel, n_row, share, 16),
        out_shape=(
            jax.ShapeDtypeStruct((share, features * BINS), jnp.float32),
            jax.ShapeDtypeStruct((share, LANES), jnp.float32),
        ),
        in_specs=[vmem(), pl.BlockSpec(memory_space=pltpu.SMEM)] + [vmem()] * n_row,
        out_specs=(vmem(), vmem()),
        scratch_shapes=[pltpu.VMEM((18 * share, n_row * rows), jnp.bfloat16)],
        name="gains",
    )(values, nbins, *bins)


def max_over(x, axis, size):
    step = 1
    while step < size:
        x = jnp.maximum(x, lax.ppermute(x, axis, [(i, i ^ step) for i in range(size)]))
        step *= 2
    return x


def on_device(n_row, n_feat, logits, labels, projection, bins, nbins, leaf):
    own = narrow(bins, leaf)
    all_bins = [own]
    for s in range(1, n_row):
        all_bins.append(lax.ppermute(own, "row", [((i + s) % n_row, i) for i in range(n_row)]))
    copies = gradient_values(logits, labels, projection, n_row * n_feat)
    values = lax.all_to_all(copies, ("row", "feat"), 0, 0)
    gain, best = split_gains(values, nbins, all_bins, n_row)
    best = max_over(best, "feat", n_feat)
    return gain / (best[:, :1] + epsilon)


def solution(mesh):
    return jax.shard_map(
        functools.partial(on_device, mesh.shape["row"], mesh.shape["feat"]),
        mesh=mesh,
        in_specs=(
            P(("row", "feat"), None),
            P(("row", "feat")),
            P(),
            P("feat", "row"),
            P("feat"),
            P("row"),
        ),
        out_specs=P("row", "feat"),
        check_vma=False,
    )
```

```python
import functools

import jax
import jax.numpy as jnp
from jax import lax
from jax.experimental import pallas as pl
from jax.experimental.pallas import tpu as pltpu
from jax.sharding import PartitionSpec as P


BINS = 64
LEAVES = 16
LANES = 128
STEPS = 4
ridge = 1.0
epsilon = 1e-06


def vmem():
    return pl.BlockSpec(memory_space=pltpu.VMEM)


def lanes_of(features):
    return features * max(1, LANES // features)


def prepare_kernel(bins_hbm, leaf_hbm, logits_hbm, labels_hbm, projection_hbm, turned_ref, values_ref, *scratch):
    bins_ref, leaf_ref, logits_ref, labels_ref, projection_ref, arrived = scratch
    pairs = (
        (logits_hbm, logits_ref),
        (labels_hbm, labels_ref),
        (projection_hbm, projection_ref),
        (bins_hbm, bins_ref),
        (leaf_hbm, leaf_ref),
    )
    arrivals = [pltpu.make_async_copy(a, b, arrived.at[i]) for i, (a, b) in enumerate(pairs)]
    for arrival in arrivals:
        arrival.start()
    for arrival in arrivals[:3]:
        arrival.wait()

    rows, classes = logits_ref.shape
    scores = logits_ref[...].astype(jnp.float32)
    highest = jnp.max(scores, axis=1, keepdims=True)
    expd = jnp.exp(scores - highest)
    probability = expd / jnp.sum(expd, axis=1, keepdims=True)
    labels = jnp.broadcast_to(labels_ref[...].astype(jnp.float32), (LANES, rows))
    labels = jnp.transpose(labels)[:, :1].astype(jnp.int32)
    lane = lax.broadcasted_iota(jnp.int32, (rows, classes), 1)
    target = jnp.where(lane == labels, 1.0, 0.0)
    gradient = (probability - target).astype(jnp.bfloat16)
    sketch = lax.dot_general(
        projection_ref[...], gradient, (((1,), (1,)), ((), ())), preferred_element_type=jnp.float32
    )
    hessian = jnp.sum(probability * (1.0 - probability), axis=1, keepdims=True)
    hessian = jnp.transpose(jnp.broadcast_to(hessian, (rows, LANES)))[:8, :]
    top = jnp.concatenate([sketch[:8], hessian], axis=0)
    low = jnp.concatenate([sketch[8:], jnp.zeros_like(hessian)], axis=0)
    packed = jnp.concatenate([top, low], axis=1).astype(jnp.bfloat16)
    values_ref[...] = jnp.broadcast_to(packed[None], values_ref.shape)

    for arrival in arrivals[3:]:
        arrival.wait()
    lines = bins_ref.shape[1]
    turned = jnp.transpose(bins_ref[...].astype(jnp.float32))
    copies = turned_ref.shape[1] // bins_ref.shape[0]
    if copies > 1:
        turned = jnp.concatenate([turned] * copies, axis=1)
    turned_ref[:lines, :] = turned.astype(jnp.bfloat16)
    leaf = leaf_ref[...].astype(jnp.float32)
    spare = turned_ref.shape[0] - lines - leaf.shape[0]
    leaf = jnp.concatenate([leaf, jnp.zeros((spare, LANES), jnp.float32)], axis=0) if spare else leaf
    turned_ref[lines:, :LANES] = leaf.astype(jnp.bfloat16)


def prepare(bins, leaf, logits, labels, projection, destinations):
    features, lines = bins.shape
    rows = logits.shape[0]
    tail = -(-lines // LANES // 16) * 16
    given = (bins, leaf.reshape(lines // LANES, LANES), logits, labels.reshape(1, rows), projection.T)
    return pl.pallas_call(
        prepare_kernel,
        out_shape=(
            jax.ShapeDtypeStruct((lines + tail, lanes_of(features)), jnp.bfloat16),
            jax.ShapeDtypeStruct((destinations, 16, 2 * rows), jnp.bfloat16),
        ),
        in_specs=[pl.BlockSpec(memory_space=pltpu.HBM)] * 5,
        out_specs=(vmem(), vmem()),
        scratch_shapes=[pltpu.VMEM(x.shape, x.dtype) for x in given] + [pltpu.SemaphoreType.DMA((5,))],
        compiler_params=pltpu.CompilerParams(vmem_limit_bytes=16 << 20),
        name="prepare",
    )(*[pltpu.with_memory_space_constraint(x, pltpu.HBM) for x in given])


def gain_kernel(n_row, share, features, steps, values_ref, nbins_ref, *refs):
    bins_refs, (gain_ref, best_ref), (weights,) = refs[:n_row], refs[n_row : n_row + 2], refs[n_row + 2 :]
    width = bins_refs[0].shape[1]
    sources = values_ref.shape[0] // n_row
    half = values_ref.shape[2] // 2
    rows = sources * half
    me = lax.axis_index("row")
    wide = (share, LANES)
    my_leaf = lax.broadcasted_iota(jnp.int32, wide, 0) + me * share
    my_leaf = my_leaf.astype(jnp.float32)
    left_half = lax.broadcasted_iota(jnp.int32, (16, LANES), 1) < half
    totals = [jnp.zeros(wide, jnp.float32) for _ in range(17)]
    for s in range(n_row):
        shard = lax.rem(me + s, n_row)
        for pair in range(sources // 2):
            first = values_ref[shard * sources + 2 * pair].astype(jnp.float32)
            second = values_ref[shard * sources + 2 * pair + 1].astype(jnp.float32)
            top = jnp.where(left_half, first, pltpu.roll(second, half, 1))
            low = jnp.where(left_half, pltpu.roll(first, half, 1), second)
            at = rows + pair // 16 * 16
            leaf = bins_refs[s][at : at + 16, :LANES].astype(jnp.float32)[pair % 16 : pair % 16 + 1]
            mine = jnp.broadcast_to(leaf, wide) == my_leaf
            pieces = []
            for k in range(17):
                row = top[k : k + 1] if k < 8 else low[k - 8 : k - 7] if k < 16 else top[8:9]
                piece = jnp.where(mine, jnp.broadcast_to(row, wide), 0.0)
                totals[k] = totals[k] + piece
                pieces.append(piece)
            spare = -(-17 * share // 16) * 16 - 17 * share
            if spare:
                pieces.append(jnp.zeros((spare, LANES), jnp.float32))
            weights[:, s * rows + pair * LANES : s * rows + (pair + 1) * LANES] = jnp.concatenate(
                pieces, axis=0
            ).astype(jnp.bfloat16)
    full = (share, width)
    totals = [jnp.broadcast_to(jnp.sum(t, axis=1, keepdims=True), full) for t in totals]

    def score(sums):
        squares = sums[0] * sums[0]
        for k in range(1, 16):
            squares = squares + sums[k] * sums[k]
        return squares / (sums[16] + ridge)

    of_all = score(totals)
    copies = width // features
    bin_of = lax.broadcasted_iota(jnp.int32, (1, width), 1) // features
    last = jnp.broadcast_to(nbins_ref[...] - 1, full)
    one, zero = jnp.bfloat16(1.0), jnp.bfloat16(0.0)

    def add_group(g, best):
        sums = None
        ids = [bin_of + (g * steps + j) * copies for j in range(steps)]
        for s in range(n_row):
            table = bins_refs[s][:rows, :]
            tables = jnp.concatenate(
                [jnp.where(table <= i.astype(jnp.float32).astype(jnp.bfloat16), one, zero) for i in ids], axis=1
            )
            part = lax.dot_general(
                weights[:, s * rows : (s + 1) * rows],
                tables,
                (((1,), (0,)), ((), ())),
                preferred_element_type=jnp.float32,
            )
            sums = part if sums is None else sums + part
        for j in range(steps):
            left = [sums[k * share : (k + 1) * share, j * width : (j + 1) * width] for k in range(17)]
            right = [totals[k] - left[k] for k in range(17)]
            gain = score(left) + score(right) - of_all
            gain = jnp.where(jnp.broadcast_to(ids[j], full) < last, gain, 0.0)
            gain_ref[g * steps + j] = gain
            best = jnp.maximum(best, gain)
        return best

    count = BINS // copies // steps
    best = lax.fori_loop(0, count, add_group, jnp.full(full, -jnp.inf, jnp.float32))
    best_ref[...] = jnp.broadcast_to(jnp.max(best, axis=1, keepdims=True), wide)


def split_gains(values, nbins, bins, n_row):
    share = LEAVES // n_row
    features = nbins.shape[0]
    width = bins[0].shape[1]
    copies = width // features
    rows = values.shape[0] // n_row * values.shape[2] // 2
    return pl.pallas_call(
        functools.partial(gain_kernel, n_row, share, features, STEPS),
        out_shape=(
            jax.ShapeDtypeStruct((BINS // copies, share, width), jnp.float32),
            jax.ShapeDtypeStruct((share, LANES), jnp.float32),
        ),
        in_specs=[vmem()] * (2 + n_row),
        out_specs=(vmem(), vmem()),
        scratch_shapes=[pltpu.VMEM((-(-17 * share // 16) * 16, n_row * rows), jnp.bfloat16)],
        compiler_params=pltpu.CompilerParams(vmem_limit_bytes=16 << 20),
        name="gains",
    )(values, jnp.tile(nbins, copies).reshape(1, width), *bins)


def max_over(x, axis, size):
    step = 1
    while step < size:
        x = jnp.maximum(x, lax.ppermute(x, axis, [(i, i ^ step) for i in range(size)]))
        step *= 2
    return x


def on_device(n_row, n_feat, logits, labels, projection, bins, nbins, leaf):
    own, copies = prepare(bins, leaf, logits, labels, projection, n_row * n_feat)
    values = lax.all_to_all(copies, ("row", "feat"), 0, 0)
    all_bins = [own]
    for s in range(1, n_row):
        all_bins.append(lax.ppermute(own, "row", [((i + s) % n_row, i) for i in range(n_row)]))
    gain, best = split_gains(values, nbins, all_bins, n_row)
    best = max_over(best, "feat", n_feat)
    share, features = best.shape[0], bins.shape[0]
    gain = gain.transpose(1, 0, 2).reshape(share, BINS, features).transpose(0, 2, 1)
    return gain.reshape(share, features * BINS) / (best[:, :1] + epsilon)


def solution(mesh):
    return jax.shard_map(
        functools.partial(on_device, mesh.shape["row"], mesh.shape["feat"]),
        mesh=mesh,
        in_specs=(
            P(("row", "feat"), None),
            P(("row", "feat")),
            P(),
            P("feat", "row"),
            P("feat"),
            P("row"),
        ),
        out_specs=P("row", "feat"),
        check_vma=False,
    )
```

```python
import functools

import jax
import jax.numpy as jnp
from jax import lax
from jax.experimental import pallas as pl
from jax.experimental.pallas import tpu as pltpu
from jax.sharding import PartitionSpec as P


BINS = 64
LEAVES = 16
LANES = 128
STEPS = 16
ridge = 1.0
epsilon = 1e-06


def vmem():
    return pl.BlockSpec(memory_space=pltpu.VMEM)


def lanes_of(features):
    return features * max(1, LANES // features)


def prepare_kernel(bins_hbm, leaf_hbm, logits_hbm, labels_hbm, projection_hbm, turned_ref, values_ref, *scratch):
    bins_ref, leaf_ref, logits_ref, labels_ref, projection_ref, arrived = scratch
    pairs = (
        (logits_hbm, logits_ref),
        (labels_hbm, labels_ref),
        (projection_hbm, projection_ref),
        (bins_hbm, bins_ref),
        (leaf_hbm, leaf_ref),
    )
    arrivals = [pltpu.make_async_copy(a, b, arrived.at[i]) for i, (a, b) in enumerate(pairs)]
    for arrival in arrivals:
        arrival.start()
    for arrival in arrivals[:3]:
        arrival.wait()

    rows, classes = logits_ref.shape
    scores = logits_ref[...].astype(jnp.float32)
    highest = jnp.max(scores, axis=1, keepdims=True)
    expd = jnp.exp(scores - highest)
    probability = expd / jnp.sum(expd, axis=1, keepdims=True)
    labels = jnp.broadcast_to(labels_ref[...].astype(jnp.float32), (LANES, rows))
    labels = jnp.transpose(labels)[:, :1].astype(jnp.int32)
    lane = lax.broadcasted_iota(jnp.int32, (rows, classes), 1)
    target = jnp.where(lane == labels, 1.0, 0.0)
    gradient = (probability - target).astype(jnp.bfloat16)
    sketch = lax.dot_general(
        projection_ref[...], gradient, (((1,), (1,)), ((), ())), preferred_element_type=jnp.float32
    )
    hessian = jnp.sum(probability * (1.0 - probability), axis=1, keepdims=True)
    hessian = jnp.transpose(jnp.broadcast_to(hessian, (rows, LANES)))[:8, :]
    top = jnp.concatenate([sketch[:8], hessian], axis=0)
    low = jnp.concatenate([sketch[8:], jnp.zeros_like(hessian)], axis=0)
    packed = jnp.concatenate([top, low], axis=1).astype(jnp.bfloat16)
    values_ref[...] = jnp.broadcast_to(packed[None], values_ref.shape)

    for arrival in arrivals[3:]:
        arrival.wait()
    lines = bins_ref.shape[1]
    turned = jnp.transpose(bins_ref[...].astype(jnp.float32))
    copies = turned_ref.shape[1] // bins_ref.shape[0]
    if copies > 1:
        turned = jnp.concatenate([turned] * copies, axis=1)
    turned_ref[:lines, :] = turned.astype(jnp.bfloat16)
    leaf = leaf_ref[...].astype(jnp.float32)
    spare = turned_ref.shape[0] - lines - leaf.shape[0]
    leaf = jnp.concatenate([leaf, jnp.zeros((spare, LANES), jnp.float32)], axis=0) if spare else leaf
    turned_ref[lines:, :LANES] = leaf.astype(jnp.bfloat16)


def prepare(bins, leaf, logits, labels, projection, destinations):
    features, lines = bins.shape
    rows = logits.shape[0]
    tail = -(-lines // LANES // 16) * 16
    given = (bins, leaf.reshape(lines // LANES, LANES), logits, labels.reshape(1, rows), projection.T)
    return pl.pallas_call(
        prepare_kernel,
        out_shape=(
            jax.ShapeDtypeStruct((lines + tail, lanes_of(features)), jnp.bfloat16),
            jax.ShapeDtypeStruct((destinations, 16, 2 * rows), jnp.bfloat16),
        ),
        in_specs=[pl.BlockSpec(memory_space=pltpu.HBM)] * 5,
        out_specs=(vmem(), vmem()),
        scratch_shapes=[pltpu.VMEM(x.shape, x.dtype) for x in given] + [pltpu.SemaphoreType.DMA((5,))],
        compiler_params=pltpu.CompilerParams(vmem_limit_bytes=16 << 20),
        name="prepare",
    )(*[pltpu.with_memory_space_constraint(x, pltpu.HBM) for x in given])


def gain_kernel(n_row, share, features, steps, values_ref, nbins_ref, *refs):
    bins_refs, (gain_ref, best_ref), (weights, wide_bins) = refs[:n_row], refs[n_row : n_row + 2], refs[n_row + 2 :]
    width = bins_refs[0].shape[1]
    sources = values_ref.shape[0] // n_row
    half = values_ref.shape[2] // 2
    rows = sources * half
    me = lax.axis_index("row")
    wide = (share, LANES)
    my_leaf = lax.broadcasted_iota(jnp.int32, wide, 0) + me * share
    my_leaf = my_leaf.astype(jnp.float32)
    left_half = lax.broadcasted_iota(jnp.int32, (16, LANES), 1) < half
    totals = [jnp.zeros(wide, jnp.float32) for _ in range(17)]
    for s in range(n_row):
        shard = lax.rem(me + s, n_row)
        for pair in range(sources // 2):
            first = values_ref[shard * sources + 2 * pair].astype(jnp.float32)
            second = values_ref[shard * sources + 2 * pair + 1].astype(jnp.float32)
            top = jnp.where(left_half, first, pltpu.roll(second, half, 1))
            low = jnp.where(left_half, pltpu.roll(first, half, 1), second)
            at = rows + pair // 16 * 16
            leaf = bins_refs[s][at : at + 16, :LANES].astype(jnp.float32)[pair % 16 : pair % 16 + 1]
            mine = jnp.broadcast_to(leaf, wide) == my_leaf
            pieces = []
            for k in range(17):
                row = top[k : k + 1] if k < 8 else low[k - 8 : k - 7] if k < 16 else top[8:9]
                piece = jnp.where(mine, jnp.broadcast_to(row, wide), 0.0)
                totals[k] = totals[k] + piece
                pieces.append(piece)
            spare = -(-17 * share // 16) * 16 - 17 * share
            if spare:
                pieces.append(jnp.zeros((spare, LANES), jnp.float32))
            weights[:, s * rows + pair * LANES : s * rows + (pair + 1) * LANES] = jnp.concatenate(
                pieces, axis=0
            ).astype(jnp.bfloat16)
        wide_bins[s * rows : (s + 1) * rows, :] = bins_refs[s][:rows, :].astype(jnp.float32)
    full = (share, width)
    totals = [jnp.broadcast_to(jnp.sum(t, axis=1, keepdims=True), full) for t in totals]

    def score(sums):
        squares = sums[0] * sums[0]
        for k in range(1, 16):
            squares = squares + sums[k] * sums[k]
        return squares / (sums[16] + ridge)

    of_all = score(totals)
    copies = width // features
    bin_of = lax.broadcasted_iota(jnp.int32, (1, width), 1) // features
    last = jnp.broadcast_to(nbins_ref[...] - 1, full)
    one, zero = jnp.bfloat16(1.0), jnp.bfloat16(0.0)

    def add_group(g, best):
        ids = [bin_of + (g * steps + j) * copies for j in range(steps)]
        table = wide_bins[...].astype(jnp.bfloat16)
        tables = jnp.concatenate(
            [jnp.where(table <= i.astype(jnp.float32).astype(jnp.bfloat16), one, zero) for i in ids], axis=1
        )
        sums = jnp.dot(weights[...], tables, preferred_element_type=jnp.float32)
        for j in range(steps):
            left = [sums[k * share : (k + 1) * share, j * width : (j + 1) * width] for k in range(17)]
            right = [totals[k] - left[k] for k in range(17)]
            gain = score(left) + score(right) - of_all
            gain = jnp.where(jnp.broadcast_to(ids[j], full) < last, gain, 0.0)
            gain_ref[g * steps + j] = gain
            best = jnp.maximum(best, gain)
        return best

    count = BINS // copies // steps
    best = lax.fori_loop(0, count, add_group, jnp.full(full, -jnp.inf, jnp.float32))
    best_ref[...] = jnp.broadcast_to(jnp.max(best, axis=1, keepdims=True), wide)


def split_gains(values, nbins, bins, n_row):
    share = LEAVES // n_row
    features = nbins.shape[0]
    width = bins[0].shape[1]
    copies = width // features
    rows = values.shape[0] // n_row * values.shape[2] // 2
    return pl.pallas_call(
        functools.partial(gain_kernel, n_row, share, features, STEPS),
        out_shape=(
            jax.ShapeDtypeStruct((BINS // copies, share, width), jnp.float32),
            jax.ShapeDtypeStruct((share, LANES), jnp.float32),
        ),
        in_specs=[vmem()] * (2 + n_row),
        out_specs=(vmem(), vmem()),
        scratch_shapes=[
            pltpu.VMEM((-(-17 * share // 16) * 16, n_row * rows), jnp.bfloat16),
            pltpu.VMEM((n_row * rows, width), jnp.float32),
        ],
        compiler_params=pltpu.CompilerParams(vmem_limit_bytes=16 << 20),
        name="gains",
    )(values, jnp.tile(nbins, copies).reshape(1, width), *bins)


def max_over(x, axis, size):
    step = 1
    while step < size:
        x = jnp.maximum(x, lax.ppermute(x, axis, [(i, i ^ step) for i in range(size)]))
        step *= 2
    return x


def on_device(n_row, n_feat, logits, labels, projection, bins, nbins, leaf):
    own, copies = prepare(bins, leaf, logits, labels, projection, n_row * n_feat)
    values = lax.all_to_all(copies, ("row", "feat"), 0, 0)
    all_bins = [own]
    for s in range(1, n_row):
        all_bins.append(lax.ppermute(own, "row", [((i + s) % n_row, i) for i in range(n_row)]))
    gain, best = split_gains(values, nbins, all_bins, n_row)
    best = max_over(best, "feat", n_feat)
    share, features = best.shape[0], bins.shape[0]
    gain = gain.transpose(1, 0, 2).reshape(share, BINS, features).transpose(0, 2, 1)
    return gain.reshape(share, features * BINS) / (best[:, :1] + epsilon)


def solution(mesh):
    return jax.shard_map(
        functools.partial(on_device, mesh.shape["row"], mesh.shape["feat"]),
        mesh=mesh,
        in_specs=(
            P(("row", "feat"), None),
            P(("row", "feat")),
            P(),
            P("feat", "row"),
            P("feat"),
            P("row"),
        ),
        out_specs=P("row", "feat"),
        check_vma=False,
    )
```

```python
import functools

import jax
import jax.numpy as jnp
from jax import lax
from jax.experimental import pallas as pl
from jax.experimental.pallas import tpu as pltpu
from jax.sharding import PartitionSpec as P


BINS = 64
LEAVES = 16
LANES = 128
STEPS = 16
ridge = 1.0
epsilon = 1e-06


def vmem():
    return pl.BlockSpec(memory_space=pltpu.VMEM)


def lanes_of(features):
    return features * max(1, LANES // features)


def prepare_kernel(*refs):
    bins_hbm, leaf_hbm, logits_hbm, labels_hbm, projection_hbm, nbins_hbm, turned_ref, values_ref, nbins_ref = refs[:9]
    bins_ref, leaf_ref, logits_ref, labels_ref, projection_ref, arrived = refs[9:]
    pairs = (
        (logits_hbm, logits_ref),
        (labels_hbm, labels_ref),
        (projection_hbm, projection_ref),
        (bins_hbm, bins_ref),
        (leaf_hbm, leaf_ref),
        (nbins_hbm, nbins_ref),
    )
    arrivals = [pltpu.make_async_copy(a, b, arrived.at[i]) for i, (a, b) in enumerate(pairs)]
    for arrival in arrivals:
        arrival.start()
    for arrival in arrivals[:3]:
        arrival.wait()

    rows, classes = logits_ref.shape
    scores = logits_ref[...].astype(jnp.float32)
    highest = jnp.max(scores, axis=1, keepdims=True)
    expd = jnp.exp(scores - highest)
    probability = expd / jnp.sum(expd, axis=1, keepdims=True)
    labels = jnp.broadcast_to(labels_ref[...].astype(jnp.float32), (LANES, rows))
    labels = jnp.transpose(labels)[:, :1].astype(jnp.int32)
    lane = lax.broadcasted_iota(jnp.int32, (rows, classes), 1)
    target = jnp.where(lane == labels, 1.0, 0.0)
    gradient = (probability - target).astype(jnp.bfloat16)
    sketch = lax.dot_general(
        projection_ref[...], gradient, (((1,), (1,)), ((), ())), preferred_element_type=jnp.float32
    )
    hessian = jnp.sum(probability * (1.0 - probability), axis=1, keepdims=True)
    hessian = jnp.transpose(jnp.broadcast_to(hessian, (rows, LANES)))[:1, :]
    top = sketch[:10]
    low = jnp.concatenate([sketch[10:], hessian, jnp.zeros((3, rows), jnp.float32)], axis=0)
    packed = jnp.concatenate([top, low], axis=1)
    odd = lax.rem(lax.axis_index("feat"), 2)
    packed = jnp.where(odd == 1, pltpu.roll(packed, rows, 1), packed).astype(jnp.bfloat16)
    for c in range(5):
        block = packed[2 * c : 2 * c + 2]
        cols = slice(c * LANES, (c + 1) * LANES)
        values_ref[:, :, cols] = jnp.broadcast_to(block[None], (values_ref.shape[0], 2, LANES))

    for arrival in arrivals[3:]:
        arrival.wait()
    lines = bins_ref.shape[1]
    turned = jnp.transpose(bins_ref[...].astype(jnp.float32))
    copies = turned_ref.shape[1] // bins_ref.shape[0]
    if copies > 1:
        turned = jnp.concatenate([turned] * copies, axis=1)
    turned_ref[:lines, :] = turned.astype(jnp.bfloat16)
    leaf = leaf_ref[...].astype(jnp.float32)
    spare = turned_ref.shape[0] - lines - leaf.shape[0]
    leaf = jnp.concatenate([leaf, jnp.zeros((spare, LANES), jnp.float32)], axis=0) if spare else leaf
    turned_ref[lines:, :LANES] = leaf.astype(jnp.bfloat16)


def prepare(bins, leaf, logits, labels, projection, nbins, destinations):
    features, lines = bins.shape
    rows = logits.shape[0]
    tail = -(-lines // LANES // 16) * 16
    width = lanes_of(features)
    counts = jnp.tile(nbins, width // features).reshape(1, width)
    given = (bins, leaf.reshape(lines // LANES, LANES), logits, labels.reshape(1, rows), projection.T, counts)
    return pl.pallas_call(
        prepare_kernel,
        out_shape=(
            jax.ShapeDtypeStruct((lines + tail, lanes_of(features)), jnp.bfloat16),
            jax.ShapeDtypeStruct((destinations, 2, 10 * rows), jnp.bfloat16),
            jax.ShapeDtypeStruct((1, width), jnp.int32),
        ),
        in_specs=[pl.BlockSpec(memory_space=pltpu.HBM)] * 6,
        out_specs=(vmem(), vmem(), vmem()),
        scratch_shapes=[pltpu.VMEM(x.shape, x.dtype) for x in given[:5]] + [pltpu.SemaphoreType.DMA((6,))],
        compiler_params=pltpu.CompilerParams(vmem_limit_bytes=16 << 20),
        name="prepare",
    )(*[pltpu.with_memory_space_constraint(x, pltpu.HBM) for x in given])


def padded(share):
    return -(-17 * share // 16) * 16


def fill_weights(share, shard, values_ref, bins_ref, weights, table):
    sources, half = values_ref.shape[0] // lax.axis_size("row"), LANES // 2
    rows = sources * half
    wide = (share, LANES)
    my_leaf = lax.broadcasted_iota(jnp.int32, wide, 0) + lax.axis_index("row") * share
    my_leaf = my_leaf.astype(jnp.float32)
    left_half = lax.broadcasted_iota(jnp.int32, (2, LANES), 1) < half
    totals = [jnp.zeros(wide, jnp.float32) for _ in range(17)]
    for pair in range(sources // 2):
        columns = [None] * 20
        for c in range(5):
            cols = slice(c * LANES, (c + 1) * LANES)
            first = values_ref[shard * sources + 2 * pair, :, cols].astype(jnp.float32)
            second = values_ref[shard * sources + 2 * pair + 1, :, cols].astype(jnp.float32)
            top = jnp.where(left_half, first, second)
            low = pltpu.roll(jnp.where(left_half, second, first), half, 1)
            columns[2 * c : 2 * c + 2] = top[:1], top[1:]
            columns[10 + 2 * c : 12 + 2 * c] = low[:1], low[1:]
        at = rows + pair // 16 * 16
        leaf = bins_ref[at : at + 16, :LANES].astype(jnp.float32)[pair % 16 : pair % 16 + 1]
        mine = jnp.broadcast_to(leaf, wide) == my_leaf
        pieces = []
        for k in range(17):
            piece = jnp.where(mine, jnp.broadcast_to(columns[k], wide), 0.0)
            totals[k] = totals[k] + piece
            pieces.append(piece)
        spare = padded(share) - 17 * share
        if spare:
            pieces.append(jnp.zeros((spare, LANES), jnp.float32))
        lines = jnp.concatenate(pieces, axis=0).astype(jnp.bfloat16)
        weights[:, pair * LANES : (pair + 1) * LANES] = lines
    table[...] = bins_ref[:rows, :].astype(jnp.float32)
    return totals


def left_sums(ids, weights, table):
    one, zero = jnp.bfloat16(1.0), jnp.bfloat16(0.0)
    bins = table[...].astype(jnp.bfloat16)
    ids = [i.astype(jnp.float32).astype(jnp.bfloat16) for i in ids]
    tables = jnp.concatenate([jnp.where(bins <= i, one, zero) for i in ids], axis=1)
    return jnp.dot(weights[...], tables, preferred_element_type=jnp.float32)


def sums_kernel(share, features, steps, shift, values_ref, bins_ref, *refs):
    n_row = lax.axis_size("row")
    earlier, (sums_ref, totals_ref, weights, table) = refs[:-4], refs[-4:]
    shard = lax.rem(lax.axis_index("row") + shift, n_row)
    totals = fill_weights(share, shard, values_ref, bins_ref, weights, table)
    for k in range(17):
        totals_ref[k] = totals[k] + earlier[1][k] if earlier else totals[k]
    width = bins_ref.shape[1]
    copies = width // features
    bin_of = lax.broadcasted_iota(jnp.int32, (1, width), 1) // features

    def add_group(g, carry):
        ids = [bin_of + (g * steps + j) * copies for j in range(steps)]
        sums = left_sums(ids, weights, table)
        for j in range(steps):
            part = sums[: 17 * share, j * width : (j + 1) * width]
            sums_ref[g * steps + j] = part + earlier[0][g * steps + j] if earlier else part
        return carry

    lax.fori_loop(0, BINS // copies // steps, add_group, 0)


def partial_sums(values, bins, share, features, shift, earlier):
    width = bins.shape[1]
    rows = values.shape[0] // lax.axis_size("row") * LANES // 2
    return pl.pallas_call(
        functools.partial(sums_kernel, share, features, STEPS, shift),
        out_shape=(
            jax.ShapeDtypeStruct((BINS * features // width, 17 * share, width), jnp.float32),
            jax.ShapeDtypeStruct((17, share, LANES), jnp.float32),
        ),
        in_specs=[vmem()] * (2 + len(earlier)),
        out_specs=(vmem(), vmem()),
        scratch_shapes=[
            pltpu.VMEM((padded(share), rows), jnp.bfloat16),
            pltpu.VMEM((rows, width), jnp.float32),
        ],
        compiler_params=pltpu.CompilerParams(vmem_limit_bytes=16 << 20),
        name="sums",
    )(values, bins, *earlier)


def gain_kernel(share, features, steps, shift, values_ref, nbins_ref, bins_ref, *refs):
    n_row = lax.axis_size("row")
    earlier, (gain_ref, best_ref, weights, table) = refs[:-4], refs[-4:]
    shard = lax.rem(lax.axis_index("row") + shift, n_row)
    totals = fill_weights(share, shard, values_ref, bins_ref, weights, table)
    width = bins_ref.shape[1]
    full = (share, width)
    if earlier:
        totals = [t + earlier[1][k] for k, t in enumerate(totals)]
    totals = [jnp.broadcast_to(jnp.sum(t, axis=1, keepdims=True), full) for t in totals]

    def score(sums):
        squares = sums[0] * sums[0]
        for k in range(1, 16):
            squares = squares + sums[k] * sums[k]
        return squares / (sums[16] + ridge)

    of_all = score(totals)
    copies = width // features
    bin_of = lax.broadcasted_iota(jnp.int32, (1, width), 1) // features
    last = jnp.broadcast_to(nbins_ref[...] - 1, full)

    def add_group(g, best):
        ids = [bin_of + (g * steps + j) * copies for j in range(steps)]
        sums = left_sums(ids, weights, table)
        for j in range(steps):
            left = [sums[k * share : (k + 1) * share, j * width : (j + 1) * width] for k in range(17)]
            if earlier:
                left = [s + earlier[0][g * steps + j, k * share : (k + 1) * share] for k, s in enumerate(left)]
            right = [totals[k] - left[k] for k in range(17)]
            gain = score(left) + score(right) - of_all
            gain = jnp.where(jnp.broadcast_to(ids[j], full) < last, gain, 0.0)
            gain_ref[g * steps + j] = gain
            best = jnp.maximum(best, gain)
        return best

    count = BINS // copies // steps
    best = lax.fori_loop(0, count, add_group, jnp.full(full, -jnp.inf, jnp.float32))
    best = jnp.broadcast_to(jnp.max(best, axis=1, keepdims=True), (share, LANES))
    mine = lax.broadcasted_iota(jnp.int32, (share, LANES), 0) == lax.broadcasted_iota(jnp.int32, (share, LANES), 1)
    best_ref[...] = jnp.max(jnp.where(mine, best, -jnp.inf), axis=0, keepdims=True)


def split_gains(values, counts, bins, share, features, shift, earlier):
    width = bins.shape[1]
    copies = width // features
    rows = values.shape[0] // lax.axis_size("row") * LANES // 2
    return pl.pallas_call(
        functools.partial(gain_kernel, share, features, STEPS, shift),
        out_shape=(
            jax.ShapeDtypeStruct((BINS // copies, share, width), jnp.float32),
            jax.ShapeDtypeStruct((1, LANES), jnp.float32),
        ),
        in_specs=[vmem()] * (3 + len(earlier)),
        out_specs=(vmem(), vmem()),
        scratch_shapes=[
            pltpu.VMEM((padded(share), rows), jnp.bfloat16),
            pltpu.VMEM((rows, width), jnp.float32),
        ],
        compiler_params=pltpu.CompilerParams(vmem_limit_bytes=16 << 20),
        name="gains",
    )(values, counts, bins, *earlier)


def max_over(x, axis, size):
    step = 1
    while step < size:
        x = jnp.maximum(x, lax.ppermute(x, axis, [(i, i ^ step) for i in range(size)]))
        step *= 2
    return x


def on_device(n_row, n_feat, logits, labels, projection, bins, nbins, leaf):
    own, copies, counts = prepare(bins, leaf, logits, labels, projection, nbins, n_row * n_feat)
    values = lax.all_to_all(copies, ("row", "feat"), 0, 0)
    all_bins = [own]
    for s in range(1, n_row):
        all_bins.append(lax.ppermute(own, "row", [((i + s) % n_row, i) for i in range(n_row)]))
    share, features = LEAVES // n_row, bins.shape[0]
    earlier = ()
    for s in range(n_row - 1):
        earlier = partial_sums(values, all_bins[s], share, features, s, earlier)
    gain, best = split_gains(values, counts, all_bins[-1], share, features, n_row - 1, earlier)
    best = max_over(best, "feat", n_feat)
    gain = gain.transpose(1, 0, 2).reshape(share, BINS, features).transpose(0, 2, 1)
    return gain.reshape(share, features * BINS) / (best[0, :share, None] + epsilon)


def solution(mesh):
    return jax.shard_map(
        functools.partial(on_device, mesh.shape["row"], mesh.shape["feat"]),
        mesh=mesh,
        in_specs=(
            P(("row", "feat"), None),
            P(("row", "feat")),
            P(),
            P("feat", "row"),
            P("feat"),
            P("row"),
        ),
        out_specs=P("row", "feat"),
        check_vma=False,
    )
```

```python
import functools

import jax
import jax.numpy as jnp
from jax import lax
from jax.experimental import pallas as pl
from jax.experimental.pallas import tpu as pltpu
from jax.sharding import PartitionSpec as P


BINS = 64
LEAVES = 16
LANES = 128
STEPS = 64
ridge = 1.0
epsilon = 1e-06


def vmem():
    return pl.BlockSpec(memory_space=pltpu.VMEM)


def lanes_of(features):
    return features * max(1, LANES // features)


def prepare_kernel(*refs):
    bins_hbm, leaf_hbm, logits_hbm, labels_hbm, projection_hbm, nbins_hbm, turned_ref, values_ref, nbins_ref = refs[:9]
    bins_ref, leaf_ref, logits_ref, labels_ref, projection_ref, arrived = refs[9:]
    pairs = (
        (logits_hbm, logits_ref),
        (labels_hbm, labels_ref),
        (projection_hbm, projection_ref),
        (bins_hbm, bins_ref),
        (leaf_hbm, leaf_ref),
        (nbins_hbm, nbins_ref),
    )
    arrivals = [pltpu.make_async_copy(a, b, arrived.at[i]) for i, (a, b) in enumerate(pairs)]
    for arrival in arrivals:
        arrival.start()
    for arrival in arrivals[:3]:
        arrival.wait()

    rows, classes = logits_ref.shape
    scores = logits_ref[...].astype(jnp.float32)
    highest = jnp.max(scores, axis=1, keepdims=True)
    expd = jnp.exp(scores - highest)
    probability = expd / jnp.sum(expd, axis=1, keepdims=True)
    labels = jnp.broadcast_to(labels_ref[...].astype(jnp.float32), (LANES, rows))
    labels = jnp.transpose(labels)[:, :1].astype(jnp.int32)
    lane = lax.broadcasted_iota(jnp.int32, (rows, classes), 1)
    target = jnp.where(lane == labels, 1.0, 0.0)
    gradient = (probability - target).astype(jnp.bfloat16)
    sketch = lax.dot_general(
        projection_ref[...], gradient, (((1,), (1,)), ((), ())), preferred_element_type=jnp.float32
    )
    hessian = jnp.sum(probability * (1.0 - probability), axis=1, keepdims=True)
    hessian = jnp.transpose(jnp.broadcast_to(hessian, (rows, LANES)))[:1, :]
    top = sketch[:10]
    low = jnp.concatenate([sketch[10:], hessian, jnp.zeros((3, rows), jnp.float32)], axis=0)
    packed = jnp.concatenate([top, low], axis=1)
    odd = lax.rem(lax.axis_index("feat"), 2)
    packed = jnp.where(odd == 1, pltpu.roll(packed, rows, 1), packed).astype(jnp.bfloat16)
    for c in range(5):
        block = packed[2 * c : 2 * c + 2]
        cols = slice(c * LANES, (c + 1) * LANES)
        values_ref[:, :, cols] = jnp.broadcast_to(block[None], (values_ref.shape[0], 2, LANES))

    for arrival in arrivals[3:]:
        arrival.wait()
    lines = bins_ref.shape[1]
    turned = jnp.transpose(bins_ref[...].astype(jnp.float32))
    copies = turned_ref.shape[1] // bins_ref.shape[0]
    if copies > 1:
        turned = jnp.concatenate([turned] * copies, axis=1)
    turned_ref[:lines, :] = turned.astype(jnp.bfloat16)
    leaf = leaf_ref[...].astype(jnp.float32)
    spare = turned_ref.shape[0] - lines - leaf.shape[0]
    leaf = jnp.concatenate([leaf, jnp.zeros((spare, LANES), jnp.float32)], axis=0) if spare else leaf
    turned_ref[lines:, :LANES] = leaf.astype(jnp.bfloat16)


def prepare(bins, leaf, logits, labels, projection, nbins, destinations):
    features, lines = bins.shape
    rows = logits.shape[0]
    tail = -(-lines // LANES // 16) * 16
    width = lanes_of(features)
    counts = jnp.tile(nbins, width // features).reshape(1, width)
    given = (bins, leaf.reshape(lines // LANES, LANES), logits, labels.reshape(1, rows), projection.T, counts)
    return pl.pallas_call(
        prepare_kernel,
        out_shape=(
            jax.ShapeDtypeStruct((lines + tail, lanes_of(features)), jnp.bfloat16),
            jax.ShapeDtypeStruct((destinations, 2, 10 * rows), jnp.bfloat16),
            jax.ShapeDtypeStruct((1, width), jnp.int32),
        ),
        in_specs=[pl.BlockSpec(memory_space=pltpu.HBM)] * 6,
        out_specs=(vmem(), vmem(), vmem()),
        scratch_shapes=[pltpu.VMEM(x.shape, x.dtype) for x in given[:5]] + [pltpu.SemaphoreType.DMA((6,))],
        compiler_params=pltpu.CompilerParams(vmem_limit_bytes=16 << 20),
        name="prepare",
    )(*[pltpu.with_memory_space_constraint(x, pltpu.HBM) for x in given])


def padded(share):
    return -(-17 * share // 16) * 16


def fill_weights(share, shard, values_ref, bins_ref, weights, table):
    sources, half = values_ref.shape[0] // lax.axis_size("row"), LANES // 2
    rows = sources * half
    wide = (share, LANES)
    my_leaf = lax.broadcasted_iota(jnp.int32, wide, 0) + lax.axis_index("row") * share
    my_leaf = my_leaf.astype(jnp.float32)
    left_half = lax.broadcasted_iota(jnp.int32, (2, LANES), 1) < half
    totals = [jnp.zeros(wide, jnp.float32) for _ in range(17)]
    for pair in range(sources // 2):
        columns = [None] * 20
        for c in range(5):
            cols = slice(c * LANES, (c + 1) * LANES)
            first = values_ref[shard * sources + 2 * pair, :, cols].astype(jnp.float32)
            second = values_ref[shard * sources + 2 * pair + 1, :, cols].astype(jnp.float32)
            top = jnp.where(left_half, first, second)
            low = pltpu.roll(jnp.where(left_half, second, first), half, 1)
            columns[2 * c : 2 * c + 2] = top[:1], top[1:]
            columns[10 + 2 * c : 12 + 2 * c] = low[:1], low[1:]
        at = rows + pair // 16 * 16
        leaf = bins_ref[at : at + 16, :LANES].astype(jnp.float32)[pair % 16 : pair % 16 + 1]
        mine = jnp.broadcast_to(leaf, wide) == my_leaf
        pieces = []
        for k in range(17):
            piece = jnp.where(mine, jnp.broadcast_to(columns[k], wide), 0.0)
            totals[k] = totals[k] + piece
            pieces.append(piece)
        spare = padded(share) - 17 * share
        if spare:
            pieces.append(jnp.zeros((spare, LANES), jnp.float32))
        lines = jnp.concatenate(pieces, axis=0).astype(jnp.bfloat16)
        weights[:, pair * LANES : (pair + 1) * LANES] = lines
    table[...] = bins_ref[:rows, :].astype(jnp.float32)
    return totals


def left_sums(ids, weights, table):
    one, zero = jnp.bfloat16(1.0), jnp.bfloat16(0.0)
    bins = table[...].astype(jnp.bfloat16)
    ids = [i.astype(jnp.float32).astype(jnp.bfloat16) for i in ids]
    tables = jnp.concatenate([jnp.where(bins <= i, one, zero) for i in ids], axis=1)
    return jnp.dot(weights[...], tables, preferred_element_type=jnp.float32)


def sums_kernel(share, features, steps, shift, values_ref, bins_ref, *refs):
    n_row = lax.axis_size("row")
    earlier, (sums_ref, totals_ref, weights, table) = refs[:-4], refs[-4:]
    shard = lax.rem(lax.axis_index("row") + shift, n_row)
    totals = fill_weights(share, shard, values_ref, bins_ref, weights, table)
    for k in range(17):
        totals_ref[k] = totals[k] + earlier[1][k] if earlier else totals[k]
    width = bins_ref.shape[1]
    copies = width // features
    bin_of = lax.broadcasted_iota(jnp.int32, (1, width), 1) // features

    def add_group(g, carry):
        ids = [bin_of + (g * steps + j) * copies for j in range(steps)]
        sums = left_sums(ids, weights, table)
        for j in range(steps):
            part = sums[: 17 * share, j * width : (j + 1) * width]
            sums_ref[g * steps + j] = part + earlier[0][g * steps + j] if earlier else part
        return carry

    lax.fori_loop(0, BINS // copies // steps, add_group, 0)


def partial_sums(values, bins, share, features, shift, earlier):
    width = bins.shape[1]
    rows = values.shape[0] // lax.axis_size("row") * LANES // 2
    return pl.pallas_call(
        functools.partial(sums_kernel, share, features, min(STEPS, BINS * features // width), shift),
        out_shape=(
            jax.ShapeDtypeStruct((BINS * features // width, 17 * share, width), jnp.float32),
            jax.ShapeDtypeStruct((17, share, LANES), jnp.float32),
        ),
        in_specs=[vmem()] * (2 + len(earlier)),
        out_specs=(vmem(), vmem()),
        scratch_shapes=[
            pltpu.VMEM((padded(share), rows), jnp.bfloat16),
            pltpu.VMEM((rows, width), jnp.float32),
        ],
        compiler_params=pltpu.CompilerParams(vmem_limit_bytes=16 << 20),
        name="sums",
    )(values, bins, *earlier)


def gain_kernel(share, features, steps, shift, values_ref, nbins_ref, bins_ref, *refs):
    n_row = lax.axis_size("row")
    earlier, (gain_ref, best_ref, weights, table) = refs[:-4], refs[-4:]
    shard = lax.rem(lax.axis_index("row") + shift, n_row)
    totals = fill_weights(share, shard, values_ref, bins_ref, weights, table)
    width = bins_ref.shape[1]
    full = (share, width)
    if earlier:
        totals = [t + earlier[1][k] for k, t in enumerate(totals)]
    totals = [jnp.broadcast_to(jnp.sum(t, axis=1, keepdims=True), full) for t in totals]

    def score(sums):
        squares = sums[0] * sums[0]
        for k in range(1, 16):
            squares = squares + sums[k] * sums[k]
        return squares / (sums[16] + ridge)

    of_all = score(totals)
    copies = width // features
    bin_of = lax.broadcasted_iota(jnp.int32, (1, width), 1) // features
    last = jnp.broadcast_to(nbins_ref[...] - 1, full)

    def add_group(g, best):
        ids = [bin_of + (g * steps + j) * copies for j in range(steps)]
        sums = left_sums(ids, weights, table)
        for j in range(steps):
            left = [sums[k * share : (k + 1) * share, j * width : (j + 1) * width] for k in range(17)]
            if earlier:
                left = [s + earlier[0][g * steps + j, k * share : (k + 1) * share] for k, s in enumerate(left)]
            right = [totals[k] - left[k] for k in range(17)]
            gain = score(left) + score(right) - of_all
            gain = jnp.where(jnp.broadcast_to(ids[j], full) < last, gain, 0.0)
            gain_ref[g * steps + j] = gain
            best = jnp.maximum(best, gain)
        return best

    count = BINS // copies // steps
    best = lax.fori_loop(0, count, add_group, jnp.full(full, -jnp.inf, jnp.float32))
    best = jnp.broadcast_to(jnp.max(best, axis=1, keepdims=True), (share, LANES))
    mine = lax.broadcasted_iota(jnp.int32, (share, LANES), 0) == lax.broadcasted_iota(jnp.int32, (share, LANES), 1)
    best_ref[...] = jnp.max(jnp.where(mine, best, -jnp.inf), axis=0, keepdims=True)


def split_gains(values, counts, bins, share, features, shift, earlier):
    width = bins.shape[1]
    copies = width // features
    rows = values.shape[0] // lax.axis_size("row") * LANES // 2
    return pl.pallas_call(
        functools.partial(gain_kernel, share, features, min(STEPS, BINS // copies), shift),
        out_shape=(
            jax.ShapeDtypeStruct((BINS // copies, share, width), jnp.float32),
            jax.ShapeDtypeStruct((1, LANES), jnp.float32),
        ),
        in_specs=[vmem()] * (3 + len(earlier)),
        out_specs=(vmem(), vmem()),
        scratch_shapes=[
            pltpu.VMEM((padded(share), rows), jnp.bfloat16),
            pltpu.VMEM((rows, width), jnp.float32),
        ],
        compiler_params=pltpu.CompilerParams(vmem_limit_bytes=16 << 20),
        name="gains",
    )(values, counts, bins, *earlier)


def max_over(x, axis, size):
    step = 1
    while step < size:
        x = jnp.maximum(x, lax.ppermute(x, axis, [(i, i ^ step) for i in range(size)]))
        step *= 2
    return x


def on_device(n_row, n_feat, logits, labels, projection, bins, nbins, leaf):
    own, copies, counts = prepare(bins, leaf, logits, labels, projection, nbins, n_row * n_feat)
    values = lax.all_to_all(copies, ("row", "feat"), 0, 0)
    all_bins = [own]
    for s in range(1, n_row):
        all_bins.append(lax.ppermute(own, "row", [((i + s) % n_row, i) for i in range(n_row)]))
    share, features = LEAVES // n_row, bins.shape[0]
    earlier = ()
    for s in range(n_row - 1):
        earlier = partial_sums(values, all_bins[s], share, features, s, earlier)
    gain, best = split_gains(values, counts, all_bins[-1], share, features, n_row - 1, earlier)
    best = max_over(best, "feat", n_feat)
    gain = gain.transpose(1, 0, 2).reshape(share, BINS, features).transpose(0, 2, 1)
    return gain.reshape(share, features * BINS) / (best[0, :share, None] + epsilon)


def solution(mesh):
    return jax.shard_map(
        functools.partial(on_device, mesh.shape["row"], mesh.shape["feat"]),
        mesh=mesh,
        in_specs=(
            P(("row", "feat"), None),
            P(("row", "feat")),
            P(),
            P("feat", "row"),
            P("feat"),
            P("row"),
        ),
        out_specs=P("row", "feat"),
        check_vma=False,
    )
```

```python
import functools

import jax
import jax.numpy as jnp
from jax import lax
from jax.experimental import pallas as pl
from jax.experimental.pallas import tpu as pltpu
from jax.sharding import PartitionSpec as P


BINS = 64
LEAVES = 16
LANES = 128
UNROLLED = 1 << 24
GRANT = 16 << 20
ridge = 1.0
epsilon = 1e-06


def vmem():
    return pl.BlockSpec(memory_space=pltpu.VMEM)


def lanes_of(features):
    return features * max(1, LANES // features)


def prepare_kernel(*refs):
    bins_hbm, leaf_hbm, logits_hbm, labels_hbm, projection_hbm, nbins_hbm, turned_ref, values_ref, nbins_ref = refs[:9]
    bins_ref, leaf_ref, logits_ref, labels_ref, projection_ref, arrived = refs[9:]
    pairs = (
        (logits_hbm, logits_ref),
        (labels_hbm, labels_ref),
        (projection_hbm, projection_ref),
        (bins_hbm, bins_ref),
        (leaf_hbm, leaf_ref),
        (nbins_hbm, nbins_ref),
    )
    arrivals = [pltpu.make_async_copy(a, b, arrived.at[i]) for i, (a, b) in enumerate(pairs)]
    for arrival in arrivals:
        arrival.start()
    for arrival in arrivals[:3]:
        arrival.wait()

    rows, classes = logits_ref.shape
    scores = logits_ref[...].astype(jnp.float32)
    highest = jnp.max(scores, axis=1, keepdims=True)
    expd = jnp.exp(scores - highest)
    probability = expd / jnp.sum(expd, axis=1, keepdims=True)
    labels = jnp.broadcast_to(labels_ref[...].astype(jnp.float32), (LANES, rows))
    labels = jnp.transpose(labels)[:, :1].astype(jnp.int32)
    lane = lax.broadcasted_iota(jnp.int32, (rows, classes), 1)
    target = jnp.where(lane == labels, 1.0, 0.0)
    gradient = (probability - target).astype(jnp.bfloat16)
    sketch = lax.dot_general(
        projection_ref[...], gradient, (((1,), (1,)), ((), ())), preferred_element_type=jnp.float32
    )
    hessian = jnp.sum(probability * (1.0 - probability), axis=1, keepdims=True)
    hessian = jnp.transpose(jnp.broadcast_to(hessian, (rows, LANES)))[:1, :]
    top = sketch[:10]
    low = jnp.concatenate([sketch[10:], hessian, jnp.zeros((3, rows), jnp.float32)], axis=0)
    packed = jnp.concatenate([top, low], axis=1)
    odd = lax.rem(lax.axis_index("feat"), 2)
    packed = jnp.where(odd == 1, pltpu.roll(packed, rows, 1), packed).astype(jnp.bfloat16)
    for c in range(5):
        block = packed[2 * c : 2 * c + 2]
        cols = slice(c * LANES, (c + 1) * LANES)
        values_ref[:, :, cols] = jnp.broadcast_to(block[None], (values_ref.shape[0], 2, LANES))

    for arrival in arrivals[3:]:
        arrival.wait()
    lines = bins_ref.shape[1]
    turned = jnp.transpose(bins_ref[...].astype(jnp.float32))
    copies = turned_ref.shape[1] // bins_ref.shape[0]
    if copies > 1:
        turned = jnp.concatenate([turned] * copies, axis=1)
    turned_ref[:lines, :] = turned.astype(jnp.bfloat16)
    leaf = leaf_ref[...].astype(jnp.float32)
    spare = turned_ref.shape[0] - lines - leaf.shape[0]
    leaf = jnp.concatenate([leaf, jnp.zeros((spare, LANES), jnp.float32)], axis=0) if spare else leaf
    turned_ref[lines:, :LANES] = leaf.astype(jnp.bfloat16)


def prepare(bins, leaf, logits, labels, projection, nbins, destinations):
    features, lines = bins.shape
    rows = logits.shape[0]
    tail = -(-lines // LANES // 16) * 16
    width = lanes_of(features)
    counts = jnp.tile(nbins, width // features).reshape(1, width)
    given = (bins, leaf.reshape(lines // LANES, LANES), logits, labels.reshape(1, rows), projection.T, counts)
    return pl.pallas_call(
        prepare_kernel,
        out_shape=(
            jax.ShapeDtypeStruct((lines + tail, lanes_of(features)), jnp.bfloat16),
            jax.ShapeDtypeStruct((destinations, 2, 10 * rows), jnp.bfloat16),
            jax.ShapeDtypeStruct((1, width), jnp.int32),
        ),
        in_specs=[pl.BlockSpec(memory_space=pltpu.HBM)] * 6,
        out_specs=(vmem(), vmem(), vmem()),
        scratch_shapes=[pltpu.VMEM(x.shape, x.dtype) for x in given[:5]] + [pltpu.SemaphoreType.DMA((6,))],
        compiler_params=pltpu.CompilerParams(vmem_limit_bytes=16 << 20),
        name="prepare",
    )(*[pltpu.with_memory_space_constraint(x, pltpu.HBM) for x in given])


def padded(share):
    return -(-17 * share // 16) * 16


def fill_weights(share, shard, values_ref, bins_ref, weights, table):
    sources, half = values_ref.shape[0] // lax.axis_size("row"), LANES // 2
    rows = sources * half
    wide = (share, LANES)
    my_leaf = lax.broadcasted_iota(jnp.int32, wide, 0) + lax.axis_index("row") * share
    my_leaf = my_leaf.astype(jnp.float32)
    left_half = lax.broadcasted_iota(jnp.int32, (2, LANES), 1) < half
    totals = [jnp.zeros(wide, jnp.float32) for _ in range(17)]
    for pair in range(sources // 2):
        columns = [None] * 20
        for c in range(5):
            cols = slice(c * LANES, (c + 1) * LANES)
            first = values_ref[shard * sources + 2 * pair, :, cols].astype(jnp.float32)
            second = values_ref[shard * sources + 2 * pair + 1, :, cols].astype(jnp.float32)
            top = jnp.where(left_half, first, second)
            low = pltpu.roll(jnp.where(left_half, second, first), half, 1)
            columns[2 * c : 2 * c + 2] = top[:1], top[1:]
            columns[10 + 2 * c : 12 + 2 * c] = low[:1], low[1:]
        at = rows + pair // 16 * 16
        leaf = bins_ref[at : at + 16, :LANES].astype(jnp.float32)[pair % 16 : pair % 16 + 1]
        mine = jnp.broadcast_to(leaf, wide) == my_leaf
        pieces = []
        for k in range(17):
            piece = jnp.where(mine, jnp.broadcast_to(columns[k], wide), 0.0)
            totals[k] = totals[k] + piece
            pieces.append(piece)
        spare = padded(share) - 17 * share
        if spare:
            pieces.append(jnp.zeros((spare, LANES), jnp.float32))
        lines = jnp.concatenate(pieces, axis=0).astype(jnp.bfloat16)
        weights[:, pair * LANES : (pair + 1) * LANES] = lines
    table[...] = bins_ref[:rows, :].astype(jnp.float32)
    return totals


def left_sums(ids, weights, table):
    one, zero = jnp.bfloat16(1.0), jnp.bfloat16(0.0)
    bins = table[...].astype(jnp.bfloat16)
    ids = [i.astype(jnp.float32).astype(jnp.bfloat16) for i in ids]
    tables = jnp.concatenate([jnp.where(bins <= i, one, zero) for i in ids], axis=1)
    return jnp.dot(weights[...], tables, preferred_element_type=jnp.float32)


def gain_kernel(share, features, steps, values_ref, nbins_ref, *refs):
    n_row = lax.axis_size("row")
    bins_refs, (gain_ref, best_ref, weights, table) = refs[:-4], refs[-4:]
    rows, width = table.shape[0] // n_row, table.shape[1]
    full = (share, width)
    totals = None
    for s in range(n_row):
        shard = lax.rem(lax.axis_index("row") + s, n_row)
        these = pl.ds(s * rows, rows)
        found = fill_weights(share, shard, values_ref, bins_refs[s], weights.at[:, these], table.at[these, :])
        totals = found if totals is None else [a + b for a, b in zip(totals, found)]
    totals = [jnp.broadcast_to(jnp.sum(t, axis=1, keepdims=True), full) for t in totals]

    def score(sums):
        squares = sums[0] * sums[0]
        for k in range(1, 16):
            squares = squares + sums[k] * sums[k]
        return squares / (sums[16] + ridge)

    of_all = score(totals)
    copies = width // features
    bin_of = lax.broadcasted_iota(jnp.int32, (1, width), 1) // features
    last = jnp.broadcast_to(nbins_ref[...] - 1, full)

    def add_group(g, best):
        ids = [bin_of + (g * steps + j) * copies for j in range(steps)]
        sums = left_sums(ids, weights, table)
        for j in range(steps):
            left = [sums[k * share : (k + 1) * share, j * width : (j + 1) * width] for k in range(17)]
            right = [totals[k] - left[k] for k in range(17)]
            gain = score(left) + score(right) - of_all
            gain = jnp.where(jnp.broadcast_to(ids[j], full) < last, gain, 0.0)
            gain_ref[g * steps + j] = gain
            best = jnp.maximum(best, gain)
        return best

    count = BINS // copies // steps
    best = lax.fori_loop(0, count, add_group, jnp.full(full, -jnp.inf, jnp.float32))
    best = jnp.broadcast_to(jnp.max(best, axis=1, keepdims=True), (share, LANES))
    mine = lax.broadcasted_iota(jnp.int32, (share, LANES), 0) == lax.broadcasted_iota(jnp.int32, (share, LANES), 1)
    best_ref[...] = jnp.max(jnp.where(mine, best, -jnp.inf), axis=0, keepdims=True)


def split_gains(values, counts, bins, share, features):
    width = bins[0].shape[1]
    copies = width // features
    rows = values.shape[0] * LANES // 2
    steps = BINS // copies
    while steps % 2 == 0 and rows * width * steps > UNROLLED:
        steps //= 2
    held = rows * (4 * width + 2 * padded(share))
    return pl.pallas_call(
        functools.partial(gain_kernel, share, features, steps),
        out_shape=(
            jax.ShapeDtypeStruct((BINS // copies, share, width), jnp.float32),
            jax.ShapeDtypeStruct((1, LANES), jnp.float32),
        ),
        in_specs=[vmem()] * (2 + len(bins)),
        out_specs=(vmem(), vmem()),
        scratch_shapes=[
            pltpu.VMEM((padded(share), rows), jnp.bfloat16),
            pltpu.VMEM((rows, width), jnp.float32),
        ],
        compiler_params=pltpu.CompilerParams(vmem_limit_bytes=GRANT + 2 * held),
        name="gains",
    )(values, counts, *bins)


def max_over(x, axis, size):
    step = 1
    while step < size:
        x = jnp.maximum(x, lax.ppermute(x, axis, [(i, i ^ step) for i in range(size)]))
        step *= 2
    return x


def on_device(n_row, n_feat, logits, labels, projection, bins, nbins, leaf):
    own, copies, counts = prepare(bins, leaf, logits, labels, projection, nbins, n_row * n_feat)
    values = lax.all_to_all(copies, ("row", "feat"), 0, 0)
    all_bins = [own]
    for s in range(1, n_row):
        all_bins.append(lax.ppermute(own, "row", [((i + s) % n_row, i) for i in range(n_row)]))
    share, features = LEAVES // n_row, bins.shape[0]
    gain, best = split_gains(values, counts, all_bins, share, features)
    best = max_over(best, "feat", n_feat)
    gain = gain.transpose(1, 0, 2).reshape(share, BINS, features).transpose(0, 2, 1)
    return gain.reshape(share, features * BINS) / (best[0, :share, None] + epsilon)


def solution(mesh):
    return jax.shard_map(
        functools.partial(on_device, mesh.shape["row"], mesh.shape["feat"]),
        mesh=mesh,
        in_specs=(
            P(("row", "feat"), None),
            P(("row", "feat")),
            P(),
            P("feat", "row"),
            P("feat"),
            P("row"),
        ),
        out_specs=P("row", "feat"),
        check_vma=False,
    )
```

```python
import functools

import jax
import jax.numpy as jnp
from jax import lax
from jax.experimental import pallas as pl
from jax.experimental.pallas import tpu as pltpu
from jax.sharding import PartitionSpec as P


BINS = 64
LEAVES = 16
LANES = 128
UNROLLED = 1 << 24
GRANT = 16 << 20
ridge = 1.0
epsilon = 1e-06


def vmem():
    return pl.BlockSpec(memory_space=pltpu.VMEM)


def lanes_of(features):
    return features * max(1, LANES // features)


def prepare_kernel(*refs):
    bins_hbm, leaf_hbm, logits_hbm, labels_hbm, projection_hbm, nbins_hbm, turned_ref, values_ref, nbins_ref = refs[:9]
    bins_ref, leaf_ref, logits_ref, labels_ref, projection_ref, arrived = refs[9:]
    pairs = (
        (logits_hbm, logits_ref),
        (labels_hbm, labels_ref),
        (projection_hbm, projection_ref),
        (bins_hbm, bins_ref),
        (leaf_hbm, leaf_ref),
        (nbins_hbm, nbins_ref),
    )
    arrivals = [pltpu.make_async_copy(a, b, arrived.at[i]) for i, (a, b) in enumerate(pairs)]
    for arrival in arrivals:
        arrival.start()
    for arrival in arrivals[:3]:
        arrival.wait()

    rows, classes = logits_ref.shape
    scores = logits_ref[...].astype(jnp.float32)
    highest = jnp.max(scores, axis=1, keepdims=True)
    expd = jnp.exp(scores - highest)
    probability = expd / jnp.sum(expd, axis=1, keepdims=True)
    labels = jnp.broadcast_to(labels_ref[...].astype(jnp.float32), (LANES, rows))
    labels = jnp.transpose(labels)[:, :1].astype(jnp.int32)
    lane = lax.broadcasted_iota(jnp.int32, (rows, classes), 1)
    target = jnp.where(lane == labels, 1.0, 0.0)
    gradient = (probability - target).astype(jnp.bfloat16)
    sketch = lax.dot_general(
        projection_ref[...], gradient, (((1,), (1,)), ((), ())), preferred_element_type=jnp.float32
    )
    hessian = jnp.sum(probability * (1.0 - probability), axis=1, keepdims=True)
    hessian = jnp.transpose(jnp.broadcast_to(hessian, (rows, LANES)))[:1, :]
    top = sketch[:10]
    low = jnp.concatenate([sketch[10:], hessian, jnp.zeros((3, rows), jnp.float32)], axis=0)
    packed = jnp.concatenate([top, low], axis=1)
    odd = lax.rem(lax.axis_index("feat"), 2)
    packed = jnp.where(odd == 1, pltpu.roll(packed, rows, 1), packed).astype(jnp.bfloat16)
    for c in range(5):
        block = packed[2 * c : 2 * c + 2]
        cols = slice(c * LANES, (c + 1) * LANES)
        values_ref[:, :, cols] = jnp.broadcast_to(block[None], (values_ref.shape[0], 2, LANES))

    for arrival in arrivals[3:]:
        arrival.wait()
    lines = bins_ref.shape[1]
    turned = jnp.transpose(bins_ref[...].astype(jnp.float32))
    copies = turned_ref.shape[1] // bins_ref.shape[0]
    if copies > 1:
        turned = jnp.concatenate([turned] * copies, axis=1)
    turned_ref[:lines, :] = turned.astype(jnp.bfloat16)
    leaf = leaf_ref[...].astype(jnp.float32)
    spare = turned_ref.shape[0] - lines - leaf.shape[0]
    leaf = jnp.concatenate([leaf, jnp.zeros((spare, LANES), jnp.float32)], axis=0) if spare else leaf
    turned_ref[lines:, :LANES] = leaf.astype(jnp.bfloat16)


def prepare(bins, leaf, logits, labels, projection, nbins, destinations):
    features, lines = bins.shape
    rows = logits.shape[0]
    tail = -(-lines // LANES // 16) * 16
    width = lanes_of(features)
    counts = jnp.tile(nbins, width // features).reshape(1, width)
    given = (bins, leaf.reshape(lines // LANES, LANES), logits, labels.reshape(1, rows), projection.T, counts)
    return pl.pallas_call(
        prepare_kernel,
        out_shape=(
            jax.ShapeDtypeStruct((lines + tail, lanes_of(features)), jnp.bfloat16),
            jax.ShapeDtypeStruct((destinations, 2, 10 * rows), jnp.bfloat16),
            jax.ShapeDtypeStruct((1, width), jnp.int32),
        ),
        in_specs=[pl.BlockSpec(memory_space=pltpu.HBM)] * 6,
        out_specs=(vmem(), vmem(), vmem()),
        scratch_shapes=[pltpu.VMEM(x.shape, x.dtype) for x in given[:5]] + [pltpu.SemaphoreType.DMA((6,))],
        compiler_params=pltpu.CompilerParams(vmem_limit_bytes=16 << 20),
        name="prepare",
    )(*[pltpu.with_memory_space_constraint(x, pltpu.HBM) for x in given])


def padded(share):
    return -(-17 * share // 16) * 16


def fill_weights(share, shard, values_ref, bins_ref, weights, table):
    sources, half = values_ref.shape[0] // lax.axis_size("row"), LANES // 2
    rows = sources * half
    wide = (share, LANES)
    my_leaf = lax.broadcasted_iota(jnp.int32, wide, 0) + lax.axis_index("row") * share
    my_leaf = my_leaf.astype(jnp.float32)
    left_half = lax.broadcasted_iota(jnp.int32, (2, LANES), 1) < half
    totals = [jnp.zeros(wide, jnp.float32) for _ in range(17)]
    for pair in range(sources // 2):
        columns = [None] * 20
        for c in range(5):
            cols = slice(c * LANES, (c + 1) * LANES)
            first = values_ref[shard * sources + 2 * pair, :, cols].astype(jnp.float32)
            second = values_ref[shard * sources + 2 * pair + 1, :, cols].astype(jnp.float32)
            top = jnp.where(left_half, first, second)
            low = pltpu.roll(jnp.where(left_half, second, first), half, 1)
            columns[2 * c : 2 * c + 2] = top[:1], top[1:]
            columns[10 + 2 * c : 12 + 2 * c] = low[:1], low[1:]
        at = rows + pair // 16 * 16
        leaf = bins_ref[at : at + 16, :LANES].astype(jnp.float32)[pair % 16 : pair % 16 + 1]
        mine = jnp.broadcast_to(leaf, wide) == my_leaf
        pieces = []
        for k in range(17):
            piece = jnp.where(mine, jnp.broadcast_to(columns[k], wide), 0.0)
            totals[k] = totals[k] + piece
            pieces.append(piece)
        spare = padded(share) - 17 * share
        if spare:
            pieces.append(jnp.zeros((spare, LANES), jnp.float32))
        lines = jnp.concatenate(pieces, axis=0).astype(jnp.bfloat16)
        weights[:, pair * LANES : (pair + 1) * LANES] = lines
    table[...] = bins_ref[:rows, :].astype(jnp.float32)
    return totals


def left_sums(ids, weights, table):
    one, zero = jnp.bfloat16(1.0), jnp.bfloat16(0.0)
    bins = table[...].astype(jnp.bfloat16)
    ids = [i.astype(jnp.float32).astype(jnp.bfloat16) for i in ids]
    tables = jnp.concatenate([jnp.where(bins <= i, one, zero) for i in ids], axis=1)
    return jnp.dot(weights[...], tables, preferred_element_type=jnp.float32)


def gain_kernel(share, features, steps, values_ref, nbins_ref, *refs):
    n_row = lax.axis_size("row")
    bins_refs, (gain_ref, best_ref, weights, table) = refs[:-4], refs[-4:]
    rows, width = table.shape[0] // n_row, table.shape[1]
    full = (share, width)
    totals = None
    for s in range(n_row):
        shard = lax.rem(lax.axis_index("row") + s, n_row)
        these = pl.ds(s * rows, rows)
        found = fill_weights(share, shard, values_ref, bins_refs[s], weights.at[:, these], table.at[these, :])
        totals = found if totals is None else [a + b for a, b in zip(totals, found)]
    totals = [jnp.broadcast_to(jnp.sum(t, axis=1, keepdims=True), full) for t in totals]

    def score(sums):
        squares = sums[0] * sums[0]
        for k in range(1, 16):
            squares = squares + sums[k] * sums[k]
        return squares / (sums[16] + ridge)

    of_all = score(totals)
    copies = width // features
    bin_of = lax.broadcasted_iota(jnp.int32, (1, width), 1) // features
    last = jnp.broadcast_to(nbins_ref[...] - 1, full)

    def add_group(g, best):
        ids = [bin_of + (g * steps + j) * copies for j in range(steps)]
        sums = left_sums(ids, weights, table)
        for j in range(steps):
            left = [sums[k * share : (k + 1) * share, j * width : (j + 1) * width] for k in range(17)]
            right = [totals[k] - left[k] for k in range(17)]
            gain = score(left) + score(right) - of_all
            gain = jnp.where(jnp.broadcast_to(ids[j], full) < last, gain, 0.0)
            gain_ref[g * steps + j] = gain
            best = jnp.maximum(best, gain)
        return best

    count = BINS // copies // steps
    best = lax.fori_loop(0, count, add_group, jnp.full(full, -jnp.inf, jnp.float32))
    best = jnp.broadcast_to(jnp.max(best, axis=1, keepdims=True), (share, LANES))
    mine = lax.broadcasted_iota(jnp.int32, (share, LANES), 0) == lax.broadcasted_iota(jnp.int32, (share, LANES), 1)
    best = jnp.max(jnp.where(mine, best, -jnp.inf), axis=0, keepdims=True)
    best_ref[...] = jnp.broadcast_to(best[None], best_ref.shape)


def split_gains(values, counts, bins, share, features, destinations):
    width = bins[0].shape[1]
    copies = width // features
    rows = values.shape[0] * LANES // 2
    steps = BINS // copies
    while steps % 2 == 0 and rows * width * steps > UNROLLED:
        steps //= 2
    held = rows * (4 * width + 2 * padded(share))
    return pl.pallas_call(
        functools.partial(gain_kernel, share, features, steps),
        out_shape=(
            jax.ShapeDtypeStruct((BINS // copies, share, width), jnp.float32),
            jax.ShapeDtypeStruct((destinations, 1, LANES), jnp.float32),
        ),
        in_specs=[vmem()] * (2 + len(bins)),
        out_specs=(vmem(), vmem()),
        scratch_shapes=[
            pltpu.VMEM((padded(share), rows), jnp.bfloat16),
            pltpu.VMEM((rows, width), jnp.float32),
        ],
        compiler_params=pltpu.CompilerParams(vmem_limit_bytes=GRANT + 2 * held),
        name="gains",
    )(values, counts, *bins)


def on_device(n_row, n_feat, logits, labels, projection, bins, nbins, leaf):
    own, copies, counts = prepare(bins, leaf, logits, labels, projection, nbins, n_row * n_feat)
    values = lax.all_to_all(copies, ("row", "feat"), 0, 0)
    all_bins = [own]
    for s in range(1, n_row):
        all_bins.append(lax.ppermute(own, "row", [((i + s) % n_row, i) for i in range(n_row)]))
    share, features = LEAVES // n_row, bins.shape[0]
    gain, best = split_gains(values, counts, all_bins, share, features, n_feat)
    gain = gain.transpose(1, 0, 2).reshape(share, BINS, features).transpose(0, 2, 1)
    gain, best = lax.optimization_barrier((gain.reshape(share, features * BINS), best))
    best = lax.all_to_all(best, "feat", 0, 0)
    return gain / (jnp.max(best, axis=(0, 1))[:share, None] + epsilon)


def solution(mesh):
    return jax.shard_map(
        functools.partial(on_device, mesh.shape["row"], mesh.shape["feat"]),
        mesh=mesh,
        in_specs=(
            P(("row", "feat"), None),
            P(("row", "feat")),
            P(),
            P("feat", "row"),
            P("feat"),
            P("row"),
        ),
        out_specs=P("row", "feat"),
        check_vma=False,
    )
```

```python
import functools

import jax
import jax.numpy as jnp
from jax import lax
from jax.experimental import pallas as pl
from jax.experimental.pallas import tpu as pltpu
from jax.sharding import PartitionSpec as P


BINS = 64
LEAVES = 16
LANES = 128
UNROLLED = 1 << 24
HALF = 38
QUARTER = 52
GRANT = 16 << 20
ridge = 1.0
epsilon = 1e-06


def vmem():
    return pl.BlockSpec(memory_space=pltpu.VMEM)


def lanes_of(features):
    return features * max(1, LANES // features)


def prepare_kernel(*refs):
    bins_hbm, leaf_hbm, logits_hbm, labels_hbm, projection_hbm, nbins_hbm, turned_ref, values_ref, nbins_ref = refs[:9]
    bins_ref, leaf_ref, logits_ref, labels_ref, projection_ref, arrived = refs[9:]
    pairs = (
        (logits_hbm, logits_ref),
        (labels_hbm, labels_ref),
        (projection_hbm, projection_ref),
        (bins_hbm, bins_ref),
        (leaf_hbm, leaf_ref),
        (nbins_hbm, nbins_ref),
    )
    arrivals = [pltpu.make_async_copy(a, b, arrived.at[i]) for i, (a, b) in enumerate(pairs)]
    for arrival in arrivals:
        arrival.start()
    for arrival in arrivals[:3]:
        arrival.wait()

    rows, classes = logits_ref.shape
    scores = logits_ref[...].astype(jnp.float32)
    highest = jnp.max(scores, axis=1, keepdims=True)
    expd = jnp.exp(scores - highest)
    probability = expd / jnp.sum(expd, axis=1, keepdims=True)
    labels = jnp.broadcast_to(labels_ref[...].astype(jnp.float32), (LANES, rows))
    labels = jnp.transpose(labels)[:, :1].astype(jnp.int32)
    lane = lax.broadcasted_iota(jnp.int32, (rows, classes), 1)
    target = jnp.where(lane == labels, 1.0, 0.0)
    gradient = (probability - target).astype(jnp.bfloat16)
    sketch = lax.dot_general(
        projection_ref[...], gradient, (((1,), (1,)), ((), ())), preferred_element_type=jnp.float32
    )
    hessian = jnp.sum(probability * (1.0 - probability), axis=1, keepdims=True)
    hessian = jnp.transpose(jnp.broadcast_to(hessian, (rows, LANES)))[:1, :]
    top = sketch[:10]
    low = jnp.concatenate([sketch[10:], hessian, jnp.zeros((3, rows), jnp.float32)], axis=0)
    packed = jnp.concatenate([top, low], axis=1)
    odd = lax.rem(lax.axis_index("feat"), 2)
    packed = jnp.where(odd == 1, pltpu.roll(packed, rows, 1), packed).astype(jnp.bfloat16)
    for c in range(5):
        block = packed[2 * c : 2 * c + 2]
        cols = slice(c * LANES, (c + 1) * LANES)
        values_ref[:, :, cols] = jnp.broadcast_to(block[None], (values_ref.shape[0], 2, LANES))

    for arrival in arrivals[3:]:
        arrival.wait()
    lines = bins_ref.shape[1]
    turned = jnp.transpose(bins_ref[...].astype(jnp.float32))
    copies = turned_ref.shape[1] // bins_ref.shape[0]
    if copies > 1:
        turned = jnp.concatenate([turned] * copies, axis=1)
    turned_ref[:lines, :] = turned.astype(jnp.bfloat16)
    leaf = leaf_ref[...].astype(jnp.float32)
    spare = turned_ref.shape[0] - lines - leaf.shape[0]
    leaf = jnp.concatenate([leaf, jnp.zeros((spare, LANES), jnp.float32)], axis=0) if spare else leaf
    turned_ref[lines:, :LANES] = leaf.astype(jnp.bfloat16)


def prepare(bins, leaf, logits, labels, projection, nbins, destinations):
    features, lines = bins.shape
    rows = logits.shape[0]
    tail = -(-lines // LANES // 16) * 16
    width = lanes_of(features)
    counts = jnp.tile(nbins, width // features).reshape(1, width)
    given = (bins, leaf.reshape(lines // LANES, LANES), logits, labels.reshape(1, rows), projection.T, counts)
    return pl.pallas_call(
        prepare_kernel,
        out_shape=(
            jax.ShapeDtypeStruct((lines + tail, lanes_of(features)), jnp.bfloat16),
            jax.ShapeDtypeStruct((destinations, 2, 10 * rows), jnp.bfloat16),
            jax.ShapeDtypeStruct((1, width), jnp.int32),
        ),
        in_specs=[pl.BlockSpec(memory_space=pltpu.HBM)] * 6,
        out_specs=(vmem(), vmem(), vmem()),
        scratch_shapes=[pltpu.VMEM(x.shape, x.dtype) for x in given[:5]] + [pltpu.SemaphoreType.DMA((6,))],
        compiler_params=pltpu.CompilerParams(vmem_limit_bytes=16 << 20),
        name="prepare",
    )(*[pltpu.with_memory_space_constraint(x, pltpu.HBM) for x in given])


def padded(share):
    return -(-17 * share // 16) * 16


def fill_weights(share, shard, values_ref, bins_ref, weights, table):
    sources, half = values_ref.shape[0] // lax.axis_size("row"), LANES // 2
    rows = sources * half
    wide = (share, LANES)
    my_leaf = lax.broadcasted_iota(jnp.int32, wide, 0) + lax.axis_index("row") * share
    my_leaf = my_leaf.astype(jnp.float32)
    left_half = lax.broadcasted_iota(jnp.int32, (2, LANES), 1) < half
    totals = [jnp.zeros(wide, jnp.float32) for _ in range(17)]
    for pair in range(sources // 2):
        columns = [None] * 20
        for c in range(5):
            cols = slice(c * LANES, (c + 1) * LANES)
            first = values_ref[shard * sources + 2 * pair, :, cols].astype(jnp.float32)
            second = values_ref[shard * sources + 2 * pair + 1, :, cols].astype(jnp.float32)
            top = jnp.where(left_half, first, second)
            low = pltpu.roll(jnp.where(left_half, second, first), half, 1)
            columns[2 * c : 2 * c + 2] = top[:1], top[1:]
            columns[10 + 2 * c : 12 + 2 * c] = low[:1], low[1:]
        at = rows + pair // 16 * 16
        leaf = bins_ref[at : at + 16, :LANES].astype(jnp.float32)[pair % 16 : pair % 16 + 1]
        mine = jnp.broadcast_to(leaf, wide) == my_leaf
        pieces = []
        for k in range(17):
            piece = jnp.where(mine, jnp.broadcast_to(columns[k], wide), 0.0)
            totals[k] = totals[k] + piece
            pieces.append(piece)
        spare = padded(share) - 17 * share
        if spare:
            pieces.append(jnp.zeros((spare, LANES), jnp.float32))
        lines = jnp.concatenate(pieces, axis=0).astype(jnp.bfloat16)
        weights[:, pair * LANES : (pair + 1) * LANES] = lines
    table[...] = bins_ref[:rows, :].astype(jnp.float32)
    return totals


def left_sums(ids, weights, tables):
    one, zero = jnp.bfloat16(1.0), jnp.bfloat16(0.0)
    bins = {id(ref): ref[...].astype(jnp.bfloat16) for ref in tables}
    ids = [i.astype(jnp.float32).astype(jnp.bfloat16) for i in ids]
    hot = [jnp.where(bins[id(ref)] <= i, one, zero) for i, ref in zip(ids, tables)]
    return jnp.dot(weights[...], jnp.concatenate(hot, axis=1), preferred_element_type=jnp.float32)


def gain_kernel(share, features, steps, values_ref, nbins_ref, *refs):
    n_row = lax.axis_size("row")
    bins_refs, (gain_ref, best_ref, weights, table, most_ref) = refs[:n_row], refs[n_row : n_row + 5]
    sorted_refs = refs[n_row + 5 :]
    rows, width = table.shape[0] // n_row, table.shape[1]
    full = (share, width)
    totals = None
    for s in range(n_row):
        shard = lax.rem(lax.axis_index("row") + s, n_row)
        these = pl.ds(s * rows, rows)
        found = fill_weights(share, shard, values_ref, bins_refs[s], weights.at[:, these], table.at[these, :])
        totals = found if totals is None else [a + b for a, b in zip(totals, found)]
    totals = [jnp.broadcast_to(jnp.sum(t, axis=1, keepdims=True), full) for t in totals]

    def score(sums):
        squares = sums[0] * sums[0]
        for k in range(1, 16):
            squares = squares + sums[k] * sums[k]
        return squares / (sums[16] + ridge)

    of_all = score(totals)
    copies = width // features
    bin_of = lax.broadcasted_iota(jnp.int32, (1, width), 1) // features
    last = jnp.broadcast_to(nbins_ref[...] - 1, full)

    def gain_of(sums, j):
        left = [sums[k * share : (k + 1) * share, j * width : (j + 1) * width] for k in range(17)]
        right = [totals[k] - left[k] for k in range(17)]
        return score(left) + score(right) - of_all

    def keep(at, ids, gain, best):
        gain = jnp.where(jnp.broadcast_to(ids, full) < last, gain, 0.0)
        gain_ref[at] = gain
        return jnp.maximum(best, gain)

    def add_group(g, best):
        ids = [bin_of + (g * steps + j) * copies for j in range(steps)]
        sums = left_sums(ids, weights, [table] * steps)
        for j in range(steps):
            best = keep(g * steps + j, ids[j], gain_of(sums, j), best)
        return best

    lowest = jnp.full(full, -jnp.inf, jnp.float32)

    def every_feature():
        most_ref[...] = lax.fori_loop(0, BINS // copies // steps, add_group, lowest)

    if not sorted_refs:
        every_feature()
    else:
        halves, quarters = sorted_refs
        square = (LANES, LANES)
        counts = jnp.broadcast_to(nbins_ref[...].astype(jnp.float32), square)
        other = jnp.transpose(counts)
        index = lax.broadcasted_iota(jnp.int32, square, 0)
        lane = lax.broadcasted_iota(jnp.int32, square, 1)
        ahead = jnp.where(other > counts, 1.0, jnp.where((other == counts) & (index < lane), 1.0, 0.0))
        rank = jnp.sum(ahead, axis=0, keepdims=True)
        turned = jnp.transpose(jnp.broadcast_to(rank, square)).astype(jnp.int32)
        rank = jnp.broadcast_to(rank.astype(jnp.int32), full)
        few = (last[:1] > HALF) & (rank[:1] >= LANES // 2) | (last[:1] > QUARTER) & (rank[:1] >= LANES // 4)
        fits = jnp.sum(jnp.where(few, 1, 0)) == 0

        @pl.when(fits)
        def _():
            bins = table[...].astype(jnp.bfloat16)
            for part, ref in ((2, halves), (4, quarters)):
                pick = jnp.where(turned == lax.rem(lane, LANES // part), 1.0, 0.0).astype(jnp.bfloat16)
                ref[...] = jnp.dot(bins, pick, preferred_element_type=jnp.float32)
            tiles = [(b, 1, table) for b in range(HALF)]
            tiles += [(b, 2, halves) for b in range(HALF, QUARTER, 2)]
            tiles += [(b, 4, quarters) for b in range(QUARTER, BINS, 4)]
            lanes = lax.broadcasted_iota(jnp.int32, (1, LANES), 1)
            ids = [b + lanes // (LANES // part) for b, part, _ in tiles]
            sums = left_sums(ids, weights, [ref for _, _, ref in tiles])
            best = lowest
            for j, (b, part, _) in enumerate(tiles):
                gain = gain_of(sums, j)
                for sub in range(part):
                    own = gain
                    if part > 1:
                        at = jnp.minimum(rank + sub * (LANES // part), LANES - 1)
                        own = jnp.take_along_axis(gain, at, axis=1, mode="promise_in_bounds")
                    best = keep(b + sub, jnp.full((1, LANES), b + sub, jnp.int32), own, best)
            most_ref[...] = best

        pl.when(jnp.logical_not(fits))(every_feature)

    best = most_ref[...]
    best = jnp.broadcast_to(jnp.max(best, axis=1, keepdims=True), (share, LANES))
    mine = lax.broadcasted_iota(jnp.int32, (share, LANES), 0) == lax.broadcasted_iota(jnp.int32, (share, LANES), 1)
    best = jnp.max(jnp.where(mine, best, -jnp.inf), axis=0, keepdims=True)
    best_ref[...] = jnp.broadcast_to(best[None], best_ref.shape)


def split_gains(values, counts, bins, share, features, destinations):
    width = bins[0].shape[1]
    copies = width // features
    rows = values.shape[0] * LANES // 2
    steps = BINS // copies
    while steps % 2 == 0 and rows * width * steps > UNROLLED:
        steps //= 2
    held = rows * (4 * width + 2 * padded(share))
    sort = features == LANES and steps == BINS
    return pl.pallas_call(
        functools.partial(gain_kernel, share, features, steps),
        out_shape=(
            jax.ShapeDtypeStruct((BINS // copies, share, width), jnp.float32),
            jax.ShapeDtypeStruct((destinations, 1, LANES), jnp.float32),
        ),
        in_specs=[vmem()] * (2 + len(bins)),
        out_specs=(vmem(), vmem()),
        scratch_shapes=[
            pltpu.VMEM((padded(share), rows), jnp.bfloat16),
            pltpu.VMEM((rows, width), jnp.float32),
            pltpu.VMEM((share, width), jnp.float32),
        ]
        + [pltpu.VMEM((rows, width), jnp.float32)] * (2 if sort else 0),
        compiler_params=pltpu.CompilerParams(vmem_limit_bytes=GRANT + 2 * held),
        name="gains",
    )(values, counts, *bins)


def on_device(n_row, n_feat, logits, labels, projection, bins, nbins, leaf):
    own, copies, counts = prepare(bins, leaf, logits, labels, projection, nbins, n_row * n_feat)
    values = lax.all_to_all(copies, ("row", "feat"), 0, 0)
    all_bins = [own]
    for s in range(1, n_row):
        all_bins.append(lax.ppermute(own, "row", [((i + s) % n_row, i) for i in range(n_row)]))
    share, features = LEAVES // n_row, bins.shape[0]
    gain, best = split_gains(values, counts, all_bins, share, features, n_feat)
    gain = gain.transpose(1, 0, 2).reshape(share, BINS, features).transpose(0, 2, 1)
    gain, best = lax.optimization_barrier((gain.reshape(share, features * BINS), best))
    best = lax.all_to_all(best, "feat", 0, 0)
    return gain / (jnp.max(best, axis=(0, 1))[:share, None] + epsilon)


def solution(mesh):
    return jax.shard_map(
        functools.partial(on_device, mesh.shape["row"], mesh.shape["feat"]),
        mesh=mesh,
        in_specs=(
            P(("row", "feat"), None),
            P(("row", "feat")),
            P(),
            P("feat", "row"),
            P("feat"),
            P("row"),
        ),
        out_specs=P("row", "feat"),
        check_vma=False,
    )
```

```python
import functools

import jax
import jax.numpy as jnp
from jax import lax
from jax.experimental import pallas as pl
from jax.experimental.pallas import tpu as pltpu
from jax.sharding import PartitionSpec as P


BINS = 64
LEAVES = 16
LANES = 128
UNROLLED = 1 << 24
HALF = 36
PARTS = 4
QUARTER = 48
GRANT = 16 << 20
ridge = 1.0
epsilon = 1e-06


def vmem():
    return pl.BlockSpec(memory_space=pltpu.VMEM)


def lanes_of(features):
    return features * max(1, LANES // features)


def prepare_kernel(*refs):
    bins_hbm, leaf_hbm, logits_hbm, labels_hbm, projection_hbm, nbins_hbm, turned_ref, values_ref, nbins_ref = refs[:9]
    bins_ref, leaf_ref, logits_ref, labels_ref, projection_ref, arrived = refs[9:]
    pairs = (
        (logits_hbm, logits_ref),
        (labels_hbm, labels_ref),
        (projection_hbm, projection_ref),
        (bins_hbm, bins_ref),
        (leaf_hbm, leaf_ref),
        (nbins_hbm, nbins_ref),
    )
    arrivals = [pltpu.make_async_copy(a, b, arrived.at[i]) for i, (a, b) in enumerate(pairs)]
    for arrival in arrivals:
        arrival.start()
    for arrival in arrivals[:3]:
        arrival.wait()

    rows, classes = logits_ref.shape
    scores = logits_ref[...].astype(jnp.float32)
    highest = jnp.max(scores, axis=1, keepdims=True)
    expd = jnp.exp(scores - highest)
    probability = expd / jnp.sum(expd, axis=1, keepdims=True)
    labels = jnp.broadcast_to(labels_ref[...].astype(jnp.float32), (LANES, rows))
    labels = jnp.transpose(labels)[:, :1].astype(jnp.int32)
    lane = lax.broadcasted_iota(jnp.int32, (rows, classes), 1)
    target = jnp.where(lane == labels, 1.0, 0.0)
    gradient = (probability - target).astype(jnp.bfloat16)
    sketch = lax.dot_general(
        projection_ref[...], gradient, (((1,), (1,)), ((), ())), preferred_element_type=jnp.float32
    )
    hessian = jnp.sum(probability * (1.0 - probability), axis=1, keepdims=True)
    hessian = jnp.transpose(jnp.broadcast_to(hessian, (rows, LANES)))[:1, :]
    top = sketch[:10]
    low = jnp.concatenate([sketch[10:], hessian, jnp.zeros((3, rows), jnp.float32)], axis=0)
    packed = jnp.concatenate([top, low], axis=1)
    odd = lax.rem(lax.axis_index("feat"), 2)
    packed = jnp.where(odd == 1, pltpu.roll(packed, rows, 1), packed).astype(jnp.bfloat16)
    for c in range(5):
        block = packed[2 * c : 2 * c + 2]
        cols = slice(c * LANES, (c + 1) * LANES)
        values_ref[:, :, cols] = jnp.broadcast_to(block[None], (values_ref.shape[0], 2, LANES))

    for arrival in arrivals[3:]:
        arrival.wait()
    lines = bins_ref.shape[1]
    turned = jnp.transpose(bins_ref[...].astype(jnp.float32))
    copies = turned_ref.shape[1] // bins_ref.shape[0]
    if copies > 1:
        turned = jnp.concatenate([turned] * copies, axis=1)
    turned_ref[:lines, :] = turned.astype(jnp.bfloat16)
    leaf = leaf_ref[...].astype(jnp.float32)
    spare = turned_ref.shape[0] - lines - leaf.shape[0]
    leaf = jnp.concatenate([leaf, jnp.zeros((spare, LANES), jnp.float32)], axis=0) if spare else leaf
    turned_ref[lines:, :LANES] = leaf.astype(jnp.bfloat16)


def prepare(bins, leaf, logits, labels, projection, nbins, destinations):
    features, lines = bins.shape
    rows = logits.shape[0]
    tail = -(-lines // LANES // 16) * 16
    width = lanes_of(features)
    counts = jnp.tile(nbins, width // features).reshape(1, width)
    given = (bins, leaf.reshape(lines // LANES, LANES), logits, labels.reshape(1, rows), projection.T, counts)
    return pl.pallas_call(
        prepare_kernel,
        out_shape=(
            jax.ShapeDtypeStruct((lines + tail, lanes_of(features)), jnp.bfloat16),
            jax.ShapeDtypeStruct((destinations, 2, 10 * rows), jnp.bfloat16),
            jax.ShapeDtypeStruct((1, width), jnp.int32),
        ),
        in_specs=[pl.BlockSpec(memory_space=pltpu.HBM)] * 6,
        out_specs=(vmem(), vmem(), vmem()),
        scratch_shapes=[pltpu.VMEM(x.shape, x.dtype) for x in given[:5]] + [pltpu.SemaphoreType.DMA((6,))],
        compiler_params=pltpu.CompilerParams(vmem_limit_bytes=16 << 20),
        name="prepare",
    )(*[pltpu.with_memory_space_constraint(x, pltpu.HBM) for x in given])


def padded(share):
    return -(-17 * share // 16) * 16


def fill_weights(share, shard, values_ref, bins_ref, weights, table):
    sources, half = values_ref.shape[0] // lax.axis_size("row"), LANES // 2
    rows = sources * half
    wide = (share, LANES)
    my_leaf = lax.broadcasted_iota(jnp.int32, wide, 0) + lax.axis_index("row") * share
    my_leaf = my_leaf.astype(jnp.float32)
    left_half = lax.broadcasted_iota(jnp.int32, (2, LANES), 1) < half
    for pair in range(sources // 2):
        columns = [None] * 20
        for c in range(5):
            cols = slice(c * LANES, (c + 1) * LANES)
            first = values_ref[shard * sources + 2 * pair, :, cols].astype(jnp.float32)
            second = values_ref[shard * sources + 2 * pair + 1, :, cols].astype(jnp.float32)
            top = jnp.where(left_half, first, second)
            low = pltpu.roll(jnp.where(left_half, second, first), half, 1)
            columns[2 * c : 2 * c + 2] = top[:1], top[1:]
            columns[10 + 2 * c : 12 + 2 * c] = low[:1], low[1:]
        at = rows + pair // 16 * 16
        leaf = bins_ref[at : at + 16, :LANES].astype(jnp.float32)[pair % 16 : pair % 16 + 1]
        mine = jnp.broadcast_to(leaf, wide) == my_leaf
        pieces = []
        for k in range(17):
            piece = jnp.where(mine, jnp.broadcast_to(columns[k], wide), 0.0)
            pieces.append(piece)
        spare = padded(share) - 17 * share
        if spare:
            pieces.append(jnp.zeros((spare, LANES), jnp.float32))
        lines = jnp.concatenate(pieces, axis=0).astype(jnp.bfloat16)
        weights[:, pair * LANES : (pair + 1) * LANES] = lines
    table[...] = bins_ref[:rows, :].astype(jnp.float32)


def left_sums(ids, weights, tables):
    one, zero = jnp.bfloat16(1.0), jnp.bfloat16(0.0)
    bins = {id(ref): ref[...].astype(jnp.bfloat16) for ref in tables}
    ids = [i.astype(jnp.float32).astype(jnp.bfloat16) for i in ids]
    hot = [jnp.where(bins[id(ref)] <= i, one, zero) for i, ref in zip(ids, tables)]
    return jnp.dot(weights[...], jnp.concatenate(hot, axis=1), preferred_element_type=jnp.float32)


def gain_kernel(share, features, steps, values_ref, nbins_ref, *refs):
    n_row = lax.axis_size("row")
    bins_refs, (gain_ref, best_ref, weights, table, most_ref) = refs[:n_row], refs[n_row : n_row + 5]
    sorted_refs = refs[n_row + 5 :]
    rows, width = table.shape[0] // n_row, table.shape[1]
    full = (share, width)
    for s in range(n_row):
        shard = lax.rem(lax.axis_index("row") + s, n_row)
        these = pl.ds(s * rows, rows)
        fill_weights(share, shard, values_ref, bins_refs[s], weights.at[:, these], table.at[these, :])

    def score(sums):
        squares = sums[0] * sums[0]
        for k in range(1, 16):
            squares = squares + sums[k] * sums[k]
        return squares / (sums[16] + ridge)

    copies = width // features
    bin_of = lax.broadcasted_iota(jnp.int32, (1, width), 1) // features
    last = jnp.broadcast_to(nbins_ref[...] - 1, full)

    def gain_of(sums, j, totals, of_all):
        left = [sums[k * share : (k + 1) * share, j * width : (j + 1) * width] for k in range(17)]
        right = [totals[k] - left[k] for k in range(17)]
        return score(left) + score(right) - of_all

    def keep(at, ids, gain, best):
        gain = jnp.where(jnp.broadcast_to(ids, full) < last, gain, 0.0)
        gain_ref[at] = gain
        return jnp.maximum(best, gain)

    def add_group(totals, of_all, g, best):
        ids = [bin_of + (g * steps + j) * copies for j in range(steps)]
        sums = left_sums(ids, weights, [table] * steps)
        for j in range(steps):
            best = keep(g * steps + j, ids[j], gain_of(sums, j, totals, of_all), best)
        return best

    lowest = jnp.full(full, -jnp.inf, jnp.float32)

    def every_feature():
        totals = []
        for k in range(17):
            line = weights[k * share : (k + 1) * share, :].astype(jnp.float32)
            totals.append(jnp.broadcast_to(jnp.sum(line, axis=1, keepdims=True), full))
        add = functools.partial(add_group, totals, score(totals))
        most_ref[...] = lax.fori_loop(0, BINS // copies // steps, add, lowest)

    if not sorted_refs:
        every_feature()
    else:
        halves, quarters = sorted_refs
        square = (LANES, LANES)
        counts = jnp.broadcast_to(nbins_ref[...].astype(jnp.float32), square)
        other = jnp.transpose(counts)
        index = lax.broadcasted_iota(jnp.int32, square, 0)
        lane = lax.broadcasted_iota(jnp.int32, square, 1)
        ahead = jnp.where(other > counts, 1.0, jnp.where((other == counts) & (index < lane), 1.0, 0.0))
        rank = jnp.sum(ahead, axis=0, keepdims=True)
        turned = jnp.transpose(jnp.broadcast_to(rank, square)).astype(jnp.int32)
        rank = jnp.broadcast_to(rank.astype(jnp.int32), full)
        few = (last[:1] > HALF) & (rank[:1] >= LANES // 2) | (last[:1] > QUARTER) & (rank[:1] >= LANES // 4)
        fits = jnp.sum(jnp.where(few, 1, 0)) == 0

        @pl.when(fits)
        def _():
            bins = table[...].astype(jnp.bfloat16)
            for part, ref in ((2, halves), (4, quarters)):
                pick = jnp.where(turned == lax.rem(lane, LANES // part), 1.0, 0.0).astype(jnp.bfloat16)
                ref[...] = jnp.dot(bins, pick, preferred_element_type=jnp.float32)
            tiles = [(b, 4, quarters) for b in range(BINS - 4, QUARTER - 1, -4)]
            tiles += [(b, 2, halves) for b in range(HALF, QUARTER, 2)]
            tiles += [(b, 1, table) for b in range(HALF)]
            lanes = lax.broadcasted_iota(jnp.int32, (1, LANES), 1)
            ids = [b + lanes // (LANES // part) for b, part, _ in tiles]
            sums = left_sums(ids, weights, [ref for _, _, ref in tiles])
            best = lowest
            every = [sums[k * share : (k + 1) * share, LANES - 1 : LANES] for k in range(17)]
            totals = [jnp.broadcast_to(t, full) for t in every]
            of_all = score(totals)
            for j, (b, part, _) in enumerate(tiles):
                gain = gain_of(sums, j, totals, of_all)
                for sub in range(part):
                    own = gain
                    if part > 1:
                        at = jnp.minimum(rank + sub * (LANES // part), LANES - 1)
                        own = jnp.take_along_axis(gain, at, axis=1, mode="promise_in_bounds")
                    best = keep(b + sub, jnp.full((1, LANES), b + sub, jnp.int32), own, best)
            most_ref[...] = best

        pl.when(jnp.logical_not(fits))(every_feature)

    best = most_ref[...]
    best = jnp.broadcast_to(jnp.max(best, axis=1, keepdims=True), (share, LANES))
    mine = lax.broadcasted_iota(jnp.int32, (share, LANES), 0) == lax.broadcasted_iota(jnp.int32, (share, LANES), 1)
    best = jnp.max(jnp.where(mine, best, -jnp.inf), axis=0, keepdims=True)
    best_ref[...] = jnp.broadcast_to(best[None], best_ref.shape)


def split_gains(values, counts, bins, share, features, destinations):
    width = bins[0].shape[1]
    copies = width // features
    rows = values.shape[0] * LANES // 2
    steps = BINS // copies
    while steps % 2 == 0 and rows * width * steps > UNROLLED:
        steps //= 2
    held = rows * (4 * width + 2 * padded(share))
    sort = features == LANES and steps == BINS
    return pl.pallas_call(
        functools.partial(gain_kernel, share, features, steps),
        out_shape=(
            jax.ShapeDtypeStruct((BINS // copies, share, width), jnp.float32),
            jax.ShapeDtypeStruct((destinations, 1, LANES), jnp.float32),
        ),
        in_specs=[vmem()] * (2 + len(bins)),
        out_specs=(vmem(), vmem()),
        scratch_shapes=[
            pltpu.VMEM((padded(share), rows), jnp.bfloat16),
            pltpu.VMEM((rows, width), jnp.float32),
            pltpu.VMEM((share, width), jnp.float32),
        ]
        + [pltpu.VMEM((rows, width), jnp.float32)] * (2 if sort else 0),
        compiler_params=pltpu.CompilerParams(vmem_limit_bytes=GRANT + 2 * held),
        name="gains",
    )(values, counts, *bins)


def finish_kernel(gain_ref, best_ref, out_hbm, turned, lines, staged, sems):
    share, features = out_hbm.shape[0], turned.shape[1]
    half = features // 2
    wide = (share, LANES)
    best = jnp.broadcast_to(jnp.max(best_ref[...], axis=0), wide)
    mine = lax.broadcasted_iota(jnp.int32, wide, 0) == lax.broadcasted_iota(jnp.int32, wide, 1)
    best = jnp.max(jnp.where(mine, best, -jnp.inf), axis=1, keepdims=True)
    divisor = jnp.broadcast_to(best + epsilon, wide)
    first = lax.broadcasted_iota(jnp.int32, (half, LANES), 1) < BINS
    for leaf in range(0, share, 2):
        both = [gain_ref[pl.ds(leaf + one, BINS, stride=share), :] for one in range(2)]
        turned[leaf // 2] = jnp.transpose(jnp.concatenate(both, axis=0))
        even, odd = (turned[leaf // 2, pl.ds(start, half, stride=2), :] for start in range(2))
        lines[pl.ds(leaf, half, stride=share), :] = jnp.where(first, even, pltpu.roll(odd, BINS, 1))
        lines[pl.ds(leaf + 1, half, stride=share), :] = jnp.where(first, pltpu.roll(even, BINS, 1), odd)
    copies = []
    for part in range(PARTS):
        for j in range(part * half // PARTS, (part + 1) * half // PARTS):
            staged[:, j * LANES : (j + 1) * LANES] = lines[j * share : (j + 1) * share, :] / divisor
        cols = pl.ds(part * half // PARTS * LANES, half // PARTS * LANES)
        copies.append(pltpu.make_async_copy(staged.at[:, cols], out_hbm.at[:, cols], sems.at[part]))
        copies[-1].start()
    for copy in copies:
        copy.wait()


def finish(gain, best, features):
    share = gain.shape[1]
    return pl.pallas_call(
        finish_kernel,
        out_shape=jax.ShapeDtypeStruct((share, features * BINS), jnp.float32),
        in_specs=[vmem(), vmem()],
        out_specs=pl.BlockSpec(memory_space=pltpu.HBM),
        scratch_shapes=[
            pltpu.VMEM((share // 2, features, LANES), jnp.float32),
            pltpu.VMEM((features // 2 * share, LANES), jnp.float32),
            pltpu.VMEM((share, features * BINS), jnp.float32),
            pltpu.SemaphoreType.DMA((PARTS,)),
        ],
        compiler_params=pltpu.CompilerParams(vmem_limit_bytes=GRANT),
        name="finish",
    )(gain.reshape(BINS * share, features), best)


def on_device(n_row, n_feat, logits, labels, projection, bins, nbins, leaf):
    own, copies, counts = prepare(bins, leaf, logits, labels, projection, nbins, n_row * n_feat)
    values = lax.all_to_all(copies, ("row", "feat"), 0, 0)
    all_bins = [own]
    for s in range(1, n_row):
        all_bins.append(lax.ppermute(own, "row", [((i + s) % n_row, i) for i in range(n_row)]))
    share, features = LEAVES // n_row, bins.shape[0]
    gain, best = split_gains(values, counts, all_bins, share, features, n_feat)
    if features == LANES == 2 * BINS and share % 8 == 0:
        return finish(gain, lax.all_to_all(best, "feat", 0, 0), features)
    gain = gain.transpose(1, 0, 2).reshape(share, BINS, features).transpose(0, 2, 1)
    gain, best = lax.optimization_barrier((gain.reshape(share, features * BINS), best))
    best = lax.all_to_all(best, "feat", 0, 0)
    return gain / (jnp.max(best, axis=(0, 1))[:share, None] + epsilon)


def solution(mesh):
    return jax.shard_map(
        functools.partial(on_device, mesh.shape["row"], mesh.shape["feat"]),
        mesh=mesh,
        in_specs=(
            P(("row", "feat"), None),
            P(("row", "feat")),
            P(),
            P("feat", "row"),
            P("feat"),
            P("row"),
        ),
        out_specs=P("row", "feat"),
        check_vma=False,
    )
```

```python
import functools

import jax
import jax.numpy as jnp
from jax import lax
from jax.experimental import pallas as pl
from jax.experimental.pallas import tpu as pltpu
from jax.sharding import PartitionSpec as P


BINS = 64
LEAVES = 16
LANES = 128
UNROLLED = 1 << 24
HALF = 38
PARTS = 4
QUARTER = 52
GRANT = 16 << 20
ridge = 1.0
epsilon = 1e-06


def vmem():
    return pl.BlockSpec(memory_space=pltpu.VMEM)


def lanes_of(features):
    return features * max(1, LANES // features)


def prepare_kernel(*refs):
    bins_hbm, leaf_hbm, logits_hbm, labels_hbm, projection_hbm, nbins_hbm, turned_ref, values_ref, nbins_ref = refs[:9]
    bins_ref, leaf_ref, logits_ref, labels_ref, projection_ref, arrived = refs[9:]
    pairs = (
        (logits_hbm, logits_ref),
        (labels_hbm, labels_ref),
        (projection_hbm, projection_ref),
        (bins_hbm, bins_ref),
        (leaf_hbm, leaf_ref),
        (nbins_hbm, nbins_ref),
    )
    arrivals = [pltpu.make_async_copy(a, b, arrived.at[i]) for i, (a, b) in enumerate(pairs)]
    for arrival in arrivals:
        arrival.start()
    for arrival in arrivals[:3]:
        arrival.wait()

    rows, classes = logits_ref.shape
    scores = logits_ref[...].astype(jnp.float32)
    highest = jnp.max(scores, axis=1, keepdims=True)
    expd = jnp.exp(scores - highest)
    for arrival in arrivals[3:]:
        arrival.wait()
    probability = expd / jnp.sum(expd, axis=1, keepdims=True)
    labels = jnp.broadcast_to(labels_ref[...].astype(jnp.float32), (LANES, rows))
    labels = jnp.transpose(labels)[:, :1].astype(jnp.int32)
    lane = lax.broadcasted_iota(jnp.int32, (rows, classes), 1)
    target = jnp.where(lane == labels, 1.0, 0.0)
    gradient = (probability - target).astype(jnp.bfloat16)
    sketch = lax.dot_general(
        projection_ref[...], gradient, (((1,), (1,)), ((), ())), preferred_element_type=jnp.float32
    )
    hessian = jnp.sum(probability * (1.0 - probability), axis=1, keepdims=True)
    hessian = jnp.transpose(jnp.broadcast_to(hessian, (rows, LANES)))[:1, :]
    top = sketch[:10]
    low = jnp.concatenate([sketch[10:], hessian, jnp.zeros((3, rows), jnp.float32)], axis=0)
    packed = jnp.concatenate([top, low], axis=1)
    odd = lax.rem(lax.axis_index("feat"), 2)
    packed = jnp.where(odd == 1, pltpu.roll(packed, rows, 1), packed).astype(jnp.bfloat16)
    for c in range(5):
        block = packed[2 * c : 2 * c + 2]
        cols = slice(c * LANES, (c + 1) * LANES)
        values_ref[:, :, cols] = jnp.broadcast_to(block[None], (values_ref.shape[0], 2, LANES))

    lines = bins_ref.shape[1]
    turned = jnp.transpose(bins_ref[...].astype(jnp.float32))
    copies = turned_ref.shape[1] // bins_ref.shape[0]
    if copies > 1:
        turned = jnp.concatenate([turned] * copies, axis=1)
    turned_ref[:lines, :] = turned.astype(jnp.bfloat16)
    leaf = leaf_ref[...].astype(jnp.float32)
    spare = turned_ref.shape[0] - lines - leaf.shape[0]
    leaf = jnp.concatenate([leaf, jnp.zeros((spare, LANES), jnp.float32)], axis=0) if spare else leaf
    turned_ref[lines:, :LANES] = leaf.astype(jnp.bfloat16)


def prepare(bins, leaf, logits, labels, projection, nbins, destinations):
    features, lines = bins.shape
    rows = logits.shape[0]
    tail = -(-lines // LANES // 16) * 16
    width = lanes_of(features)
    counts = jnp.tile(nbins, width // features).reshape(1, width)
    given = (bins, leaf.reshape(lines // LANES, LANES), logits, labels.reshape(1, rows), projection.T, counts)
    return pl.pallas_call(
        prepare_kernel,
        out_shape=(
            jax.ShapeDtypeStruct((lines + tail, lanes_of(features)), jnp.bfloat16),
            jax.ShapeDtypeStruct((destinations, 2, 10 * rows), jnp.bfloat16),
            jax.ShapeDtypeStruct((1, width), jnp.int32),
        ),
        in_specs=[pl.BlockSpec(memory_space=pltpu.HBM)] * 6,
        out_specs=(vmem(), vmem(), vmem()),
        scratch_shapes=[pltpu.VMEM(x.shape, x.dtype) for x in given[:5]] + [pltpu.SemaphoreType.DMA((6,))],
        compiler_params=pltpu.CompilerParams(vmem_limit_bytes=16 << 20),
        name="prepare",
    )(*[pltpu.with_memory_space_constraint(x, pltpu.HBM) for x in given])


def padded(share):
    return -(-17 * share // 16) * 16


def fill_weights(share, shard, values_ref, bins_ref, weights, table):
    sources, half = values_ref.shape[0] // lax.axis_size("row"), LANES // 2
    rows = sources * half
    wide = (share, LANES)
    my_leaf = lax.broadcasted_iota(jnp.int32, wide, 0) + lax.axis_index("row") * share
    my_leaf = my_leaf.astype(jnp.float32)
    left_half = lax.broadcasted_iota(jnp.int32, (2, LANES), 1) < half
    for pair in range(sources // 2):
        columns = [None] * 20
        for c in range(5):
            cols = slice(c * LANES, (c + 1) * LANES)
            first = values_ref[shard * sources + 2 * pair, :, cols].astype(jnp.float32)
            second = values_ref[shard * sources + 2 * pair + 1, :, cols].astype(jnp.float32)
            top = jnp.where(left_half, first, second)
            low = pltpu.roll(jnp.where(left_half, second, first), half, 1)
            columns[2 * c : 2 * c + 2] = top[:1], top[1:]
            columns[10 + 2 * c : 12 + 2 * c] = low[:1], low[1:]
        at = rows + pair // 16 * 16
        leaf = bins_ref[at : at + 16, :LANES].astype(jnp.float32)[pair % 16 : pair % 16 + 1]
        mine = jnp.broadcast_to(leaf, wide) == my_leaf
        pieces = []
        for k in range(17):
            piece = jnp.where(mine, jnp.broadcast_to(columns[k], wide), 0.0)
            pieces.append(piece)
        spare = padded(share) - 17 * share
        if spare:
            pieces.append(jnp.zeros((spare, LANES), jnp.float32))
        lines = jnp.concatenate(pieces, axis=0).astype(jnp.bfloat16)
        weights[:, pair * LANES : (pair + 1) * LANES] = lines
    table[...] = bins_ref[:rows, :].astype(jnp.float32)


def left_sums(ids, weights, tables):
    one, zero = jnp.bfloat16(1.0), jnp.bfloat16(0.0)
    bins = {id(ref): ref[...].astype(jnp.bfloat16) for ref in tables}
    ids = [i.astype(jnp.float32).astype(jnp.bfloat16) for i in ids]
    hot = [jnp.where(bins[id(ref)] <= i, one, zero) for i, ref in zip(ids, tables)]
    return jnp.dot(weights[...], jnp.concatenate(hot, axis=1), preferred_element_type=jnp.float32)


def gain_kernel(share, features, steps, values_ref, nbins_ref, *refs):
    n_row = lax.axis_size("row")
    bins_refs, (gain_ref, best_ref, weights, table, most_ref) = refs[:n_row], refs[n_row : n_row + 5]
    sorted_refs = refs[n_row + 5 :]
    rows, width = table.shape[0] // n_row, table.shape[1]
    full = (share, width)
    for s in range(n_row):
        shard = lax.rem(lax.axis_index("row") + s, n_row)
        these = pl.ds(s * rows, rows)
        fill_weights(share, shard, values_ref, bins_refs[s], weights.at[:, these], table.at[these, :])

    def score(sums):
        squares = sums[0] * sums[0]
        for k in range(1, 16):
            squares = squares + sums[k] * sums[k]
        return squares / (sums[16] + ridge)

    copies = width // features
    bin_of = lax.broadcasted_iota(jnp.int32, (1, width), 1) // features
    last = jnp.broadcast_to(nbins_ref[...] - 1, full)

    def gain_of(sums, j, totals, of_all):
        left = [sums[k * share : (k + 1) * share, j * width : (j + 1) * width] for k in range(17)]
        right = [totals[k] - left[k] for k in range(17)]
        return score(left) + score(right) - of_all

    def keep(at, ids, gain, best):
        gain = jnp.where(jnp.broadcast_to(ids, full) < last, gain, 0.0)
        gain_ref[at] = gain
        return jnp.maximum(best, gain)

    def add_group(totals, of_all, g, best):
        ids = [bin_of + (g * steps + j) * copies for j in range(steps)]
        sums = left_sums(ids, weights, [table] * steps)
        for j in range(steps):
            best = keep(g * steps + j, ids[j], gain_of(sums, j, totals, of_all), best)
        return best

    lowest = jnp.full(full, -jnp.inf, jnp.float32)

    def every_feature():
        totals = []
        for k in range(17):
            line = weights[k * share : (k + 1) * share, :].astype(jnp.float32)
            totals.append(jnp.broadcast_to(jnp.sum(line, axis=1, keepdims=True), full))
        add = functools.partial(add_group, totals, score(totals))
        most_ref[...] = lax.fori_loop(0, BINS // copies // steps, add, lowest)

    if not sorted_refs:
        every_feature()
    else:
        halves, quarters = sorted_refs
        square = (LANES, LANES)
        counts = jnp.broadcast_to(nbins_ref[...].astype(jnp.float32), square)
        other = jnp.transpose(counts)
        index = lax.broadcasted_iota(jnp.int32, square, 0)
        lane = lax.broadcasted_iota(jnp.int32, square, 1)
        ahead = jnp.where(other > counts, 1.0, jnp.where((other == counts) & (index < lane), 1.0, 0.0))
        rank = jnp.sum(ahead, axis=0, keepdims=True)
        turned = jnp.transpose(jnp.broadcast_to(rank, square)).astype(jnp.int32)
        rank = jnp.broadcast_to(rank.astype(jnp.int32), full)
        few = (last[:1] > HALF) & (rank[:1] >= LANES // 2) | (last[:1] > QUARTER) & (rank[:1] >= LANES // 4)
        fits = jnp.sum(jnp.where(few, 1, 0)) == 0

        @pl.when(fits)
        def _():
            picks = [jnp.where(turned == lax.rem(lane, LANES // part), 1.0, 0.0) for part in (2, 4)]
            picks = jnp.concatenate(picks, axis=1).astype(jnp.bfloat16)
            for s in range(n_row):
                these = slice(s * rows, (s + 1) * rows)
                bins = table[these, :].astype(jnp.bfloat16)
                picked = jnp.dot(bins, picks, preferred_element_type=jnp.float32)
                halves[these, :], quarters[these, :] = picked[:, :LANES], picked[:, LANES:]
            tiles = [(b, 4, quarters) for b in range(BINS - 4, QUARTER - 1, -4)]
            tiles += [(b, 2, halves) for b in range(HALF, QUARTER, 2)]
            tiles += [(b, 1, table) for b in range(HALF)]
            lanes = lax.broadcasted_iota(jnp.int32, (1, LANES), 1)
            ids = [b + lanes // (LANES // part) for b, part, _ in tiles]
            sums = left_sums(ids, weights, [ref for _, _, ref in tiles])
            best = lowest
            every = [sums[k * share : (k + 1) * share, LANES - 1 : LANES] for k in range(17)]
            totals = [jnp.broadcast_to(t, full) for t in every]
            of_all = score(totals)
            for j, (b, part, _) in enumerate(tiles):
                gain = gain_of(sums, j, totals, of_all)
                for sub in range(part):
                    own = gain
                    if part > 1:
                        at = jnp.minimum(rank + sub * (LANES // part), LANES - 1)
                        own = jnp.take_along_axis(gain, at, axis=1, mode="promise_in_bounds")
                    best = keep(b + sub, jnp.full((1, LANES), b + sub, jnp.int32), own, best)
            most_ref[...] = best

        pl.when(jnp.logical_not(fits))(every_feature)

    best = most_ref[...]
    best = jnp.broadcast_to(jnp.max(best, axis=1, keepdims=True), (share, LANES))
    mine = lax.broadcasted_iota(jnp.int32, (share, LANES), 0) == lax.broadcasted_iota(jnp.int32, (share, LANES), 1)
    best = jnp.max(jnp.where(mine, best, -jnp.inf), axis=0, keepdims=True)
    best_ref[...] = jnp.broadcast_to(best[None], best_ref.shape)


def split_gains(values, counts, bins, share, features, destinations):
    width = bins[0].shape[1]
    copies = width // features
    rows = values.shape[0] * LANES // 2
    steps = BINS // copies
    while steps % 2 == 0 and rows * width * steps > UNROLLED:
        steps //= 2
    held = rows * (4 * width + 2 * padded(share))
    sort = features == LANES and steps == BINS
    return pl.pallas_call(
        functools.partial(gain_kernel, share, features, steps),
        out_shape=(
            jax.ShapeDtypeStruct((BINS // copies, share, width), jnp.float32),
            jax.ShapeDtypeStruct((destinations, 1, LANES), jnp.float32),
        ),
        in_specs=[vmem()] * (2 + len(bins)),
        out_specs=(vmem(), vmem()),
        scratch_shapes=[
            pltpu.VMEM((padded(share), rows), jnp.bfloat16),
            pltpu.VMEM((rows, width), jnp.float32),
            pltpu.VMEM((share, width), jnp.float32),
        ]
        + [pltpu.VMEM((rows, width), jnp.float32)] * (2 if sort else 0),
        compiler_params=pltpu.CompilerParams(vmem_limit_bytes=GRANT + 2 * held),
        name="gains",
    )(values, counts, *bins)


def finish_kernel(gain_ref, best_ref, out_hbm, turned, lines, staged, sems):
    share, features = out_hbm.shape[0], turned.shape[1]
    half = features // 2
    wide = (share, LANES)
    best = jnp.broadcast_to(jnp.max(best_ref[...], axis=0), wide)
    mine = lax.broadcasted_iota(jnp.int32, wide, 0) == lax.broadcasted_iota(jnp.int32, wide, 1)
    best = jnp.max(jnp.where(mine, best, -jnp.inf), axis=1, keepdims=True)
    divisor = jnp.broadcast_to(best + epsilon, wide)
    first = lax.broadcasted_iota(jnp.int32, (half, LANES), 1) < BINS
    for leaf in range(0, share, 2):
        both = [gain_ref[pl.ds(leaf + one, BINS, stride=share), :] for one in range(2)]
        turned[leaf // 2] = jnp.transpose(jnp.concatenate(both, axis=0))
        even, odd = (turned[leaf // 2, pl.ds(start, half, stride=2), :] for start in range(2))
        lines[pl.ds(leaf, half, stride=share), :] = jnp.where(first, even, pltpu.roll(odd, BINS, 1))
        lines[pl.ds(leaf + 1, half, stride=share), :] = jnp.where(first, pltpu.roll(even, BINS, 1), odd)
    copies = []
    for part in range(PARTS):
        for j in range(part * half // PARTS, (part + 1) * half // PARTS):
            staged[:, j * LANES : (j + 1) * LANES] = lines[j * share : (j + 1) * share, :] / divisor
        cols = pl.ds(part * half // PARTS * LANES, half // PARTS * LANES)
        copies.append(pltpu.make_async_copy(staged.at[:, cols], out_hbm.at[:, cols], sems.at[part]))
        copies[-1].start()
    for copy in copies:
        copy.wait()


def finish(gain, best, features):
    share = gain.shape[1]
    return pl.pallas_call(
        finish_kernel,
        out_shape=jax.ShapeDtypeStruct((share, features * BINS), jnp.float32),
        in_specs=[vmem(), vmem()],
        out_specs=pl.BlockSpec(memory_space=pltpu.HBM),
        scratch_shapes=[
            pltpu.VMEM((share // 2, features, LANES), jnp.float32),
            pltpu.VMEM((features // 2 * share, LANES), jnp.float32),
            pltpu.VMEM((share, features * BINS), jnp.float32),
            pltpu.SemaphoreType.DMA((PARTS,)),
        ],
        compiler_params=pltpu.CompilerParams(vmem_limit_bytes=GRANT),
        name="finish",
    )(gain.reshape(BINS * share, features), best)


def on_device(n_row, n_feat, logits, labels, projection, bins, nbins, leaf):
    own, copies, counts = prepare(bins, leaf, logits, labels, projection, nbins, n_row * n_feat)
    values = lax.all_to_all(copies, ("row", "feat"), 0, 0)
    all_bins = [own]
    for s in range(1, n_row):
        all_bins.append(lax.ppermute(own, "row", [((i + s) % n_row, i) for i in range(n_row)]))
    share, features = LEAVES // n_row, bins.shape[0]
    gain, best = split_gains(values, counts, all_bins, share, features, n_feat)
    if features == LANES == 2 * BINS and share % 8 == 0:
        return finish(gain, lax.all_to_all(best, "feat", 0, 0), features)
    gain = gain.transpose(1, 0, 2).reshape(share, BINS, features).transpose(0, 2, 1)
    gain, best = lax.optimization_barrier((gain.reshape(share, features * BINS), best))
    best = lax.all_to_all(best, "feat", 0, 0)
    return gain / (jnp.max(best, axis=(0, 1))[:share, None] + epsilon)


def solution(mesh):
    return jax.shard_map(
        functools.partial(on_device, mesh.shape["row"], mesh.shape["feat"]),
        mesh=mesh,
        in_specs=(
            P(("row", "feat"), None),
            P(("row", "feat")),
            P(),
            P("feat", "row"),
            P("feat"),
            P("row"),
        ),
        out_specs=P("row", "feat"),
        check_vma=False,
    )
```
